32 devices in a mesh: row: 8 (over z, x), col: 4 (over y, core).
Axes of the slice: x: 2, y: 2, z: 4, core: 2. Of those that a mesh axis runs over, the one named last changes fastest.
Arguments:
- src_points: bfloat16 [64, 8192], P(None, ('row', 'col')), may hold values from -24 to 24
- tgt_points: bfloat16 [64, 4096], P(None, ('col', 'row')), may hold values from -24 to 24
- grad_f: float32 [8192], P('row'), may hold values from -6 to 6
- grad_g: float32 [4096], P('col'), may hold values from -6 to 6
Outputs:
- grad_src: float32 [64, 8192], P(None, ('row', 'col'))
- grad_tgt: float32 [64, 4096], P(None, ('col', 'row'))
The draws below stay inside these ranges and needn't reach their ends.
All inputs are finite; a program needn't handle non-finite values.
Results may differ from the reference program's by a relative error of at most 0.0085.
Values may be sent and summed in bfloat16 or wider, within the bound.
No kernel may reach another device: no remote copies, remote signals or barrier semaphores. Data moves between devices by JAX's collectives and lax.ppermute only.
A program may use at most 64 MiB of HBM per device.

```python
import math
import jax
import jax.numpy as jnp
from jax import lax

F = 64
PTS = 1024
SINK = 2
CG = 3
N = 8192
M = 4096


def scaled_points(key, count):
    base = jax.random.normal(key, (F, count), jnp.float32)
    return jnp.clip(base, -24.0, 24.0).astype(jnp.bfloat16)


def draw_src_points(key, part):
    return scaled_points(jax.random.fold_in(key, 101), N)


def draw_tgt_points(key, part):
    return scaled_points(jax.random.fold_in(key, 202), M)


def level_of(stream_key, extent, cuts, least, high):
    def one(dim, shards_of):
        steps = jax.random.uniform(jax.random.fold_in(jax.random.fold_in(stream_key, 6), dim), (shards_of,), jnp.float32, least / len(cuts), high / len(cuts))
        return jnp.repeat(jnp.exp(steps), extent[dim] // shards_of).reshape((-1,) + (1,) * (len(extent) - dim - 1))

    factor_of = one(*cuts[0])
    for cut in cuts[1:]:
        factor_of = factor_of * one(*cut)
    return factor_of


def gaussian(key, dims, scale, most, cuts=(), kind=jnp.bfloat16):
    drawn = scale * jax.random.normal(key, dims, jnp.float32)
    if cuts:
        drawn = drawn * level_of(key, dims, cuts, -0.22, 0.18)
    return jnp.clip(drawn, -most, most).astype(kind)


def setup_inputs(seed: int = 0) -> dict:
    seeds = jax.random.split(jax.random.key(seed), 5)
    return {
        "src_points": draw_src_points(jax.random.fold_in(seeds[4], 71), 0),
        "tgt_points": draw_tgt_points(jax.random.fold_in(seeds[4], 71), 0),
        "grad_f": gaussian(seeds[2], (N,), 1.0, 6.0, ((0, 8),), jnp.float32),
        "grad_g": gaussian(seeds[3], (M,), 1.0, 6.0, ((0, 4),), jnp.float32),
    }


EPS = 4.0
TAU = 0.1


def cost_tile(block_pts, block_sq, points_col, sq_col):
    cross = lax.dot_general(block_pts, points_col, (((0,), (0,)), ((), ())), preferred_element_type=jnp.float32)
    return block_sq[:, None] + sq_col[None, :] - 2.0 * cross


def reference(src_points, tgt_points, grad_f, grad_g):
    features, n_total = src_points.shape
    m_total = tgt_points.shape[1]
    block = min(512, PTS)
    block_count = n_total // block
    sq_row = jnp.sum(jnp.square(src_points.astype(jnp.float32)), axis=0)
    sq_col = jnp.sum(jnp.square(tgt_points.astype(jnp.float32)), axis=0)
    blocks_pts = jnp.moveaxis(src_points.reshape(features, block_count, block), 1, 0)
    blocks_sq = sq_row.reshape(block_count, block)
    shift = EPS * math.log(n_total / m_total)
    pot_col = jnp.zeros((m_total,), jnp.float32)
    pot_row = jnp.zeros((n_total,), jnp.float32)
    for iteration in range(SINK):
        def row_part(pieces):
            values = (pot_col[None, :] - cost_tile(pieces[0], pieces[1], tgt_points, sq_col)) / EPS
            highest = jnp.max(values, axis=1)
            return highest + jnp.log(jnp.sum(jnp.exp(values - highest[:, None]), axis=1))

        pot_row = -EPS * lax.map(row_part, (blocks_pts, blocks_sq)).reshape(-1)

        def col_part(carry, pieces):
            values = (pieces[2][:, None] - cost_tile(pieces[0], pieces[1], tgt_points, sq_col)) / EPS
            highest = jnp.maximum(carry[0], jnp.max(values, axis=0))
            totals = carry[1] * jnp.exp(carry[0] - highest) + jnp.sum(jnp.exp(values - highest[None, :]), axis=0)
            return (highest, totals), None

        start = (jnp.full((m_total,), -jnp.inf, jnp.float32), jnp.zeros((m_total,), jnp.float32))
        (highest, totals), unused = lax.scan(col_part, start, (blocks_pts, blocks_sq, pot_row.reshape(block_count, block)))
        pot_col = shift - EPS * (highest + jnp.log(totals))

    def plan_rows(pieces):
        cost = cost_tile(pieces[0], pieces[1], tgt_points, sq_col)
        return jnp.exp((pieces[2][:, None] + pot_col[None, :] - cost) / EPS).astype(jnp.bfloat16)

    plan_tile = lax.map(plan_rows, (blocks_pts, blocks_sq, pot_row.reshape(block_count, block))).reshape(n_total, m_total)
    row_mass = jnp.sum(plan_tile, axis=1, dtype=jnp.float32)
    col_mass = jnp.sum(plan_tile, axis=0, dtype=jnp.float32)

    def row_dot(vector):
        return jnp.sum(plan_tile * vector[None, :], axis=1)

    def col_dot(vector):
        return jnp.sum(plan_tile * vector[:, None], axis=0)

    def schur(vector):
        return (1.0 + TAU) * col_mass * vector - col_dot(row_dot(vector) / row_mass)

    rhs = grad_g - col_dot(grad_f / row_mass)
    dual_col = jnp.zeros_like(rhs)
    residual = rhs
    direction = rhs
    norm_now = jnp.sum(residual * residual)
    for iteration in range(CG):
        image = schur(direction)
        alpha = norm_now / jnp.sum(direction * image)
        dual_col = dual_col + alpha * direction
        residual = residual - alpha * image
        norm_next = jnp.sum(residual * residual)
        direction = residual + (norm_next / norm_now) * direction
        norm_now = norm_next
    dual_row = (grad_f - row_dot(dual_col)) / row_mass
    weights = (plan_tile * (dual_row[:, None] + dual_col[None, :])).astype(jnp.bfloat16)
    rows_w = jnp.sum(weights, axis=1, dtype=jnp.float32)
    cols_w = jnp.sum(weights, axis=0, dtype=jnp.float32)
    pulled_src = lax.dot_general(tgt_points, weights, (((1,), (1,)), ((), ())), preferred_element_type=jnp.float32)
    pulled_tgt = lax.dot_general(src_points, weights, (((1,), (0,)), ((), ())), preferred_element_type=jnp.float32)
    grad_src = 2.0 * (src_points.astype(jnp.float32) * rows_w[None, :] - pulled_src)
    grad_tgt = 2.0 * (tgt_points.astype(jnp.float32) * cols_w[None, :] - pulled_tgt)
    return grad_src, grad_tgt
```

```python
import functools
import math

import jax
import jax.numpy as jnp
from jax import lax
from jax.experimental import pallas as pl
from jax.experimental.pallas import tpu as pltpu
from jax.sharding import PartitionSpec as P

CG = 3
EPS = 4.0
TAU = 0.1
AXES = ("row", "col")
LOW = -3.0e38
LOG2E = math.log2(math.e)
CROSS = 2.0 * LOG2E / EPS
SQUARE = LOG2E / EPS
F32 = jnp.float32
BF16 = jnp.bfloat16
NT = (((1,), (1,)), ((), ()))
VMEM = pl.BlockSpec(memory_space=pltpu.VMEM)
SMEM = pl.BlockSpec(memory_space=pltpu.SMEM)


def split3(vector):
    high = vector.astype(BF16).astype(F32)
    rest = vector - high
    mid = rest.astype(BF16).astype(F32)
    low = rest - mid
    shape = (8, vector.shape[1])
    line = lax.broadcasted_iota(jnp.int32, shape, 0)
    zero = jnp.zeros(shape, F32)
    rows = jnp.where(line == 0, high, jnp.where(line == 1, mid, jnp.where(line == 2, low, zero)))
    return rows.astype(BF16)


def total(vector):
    return jnp.sum(vector, axis=1, keepdims=True)


def fold(rows):
    return jnp.sum(rows, axis=0, keepdims=True)


def down(vector):
    return jnp.broadcast_to(vector, (128, vector.shape[1])).T


def lse_kernel(group, cols, me_ref, x_ref, y_ref, xt_ref, yc_ref, sq_ref, r_ref, lse_ref, s_ref, mj_ref, lj_ref):
    me = me_ref[0]
    replicas, features, ns = x_ref.shape
    devices, _, nt = y_ref.shape
    wide = devices * nt
    for k in range(replicas):
        xt_ref[k * ns : (k + 1) * ns, :] = x_ref[k].T
    for t in range(devices):
        k = jnp.bitwise_xor(t, me)
        inner = k % group
        place = (inner % 2) * (devices // 2) + (inner // 2) * replicas + k // group
        yc_ref[:features, t * nt : (t + 1) * nt] = y_ref[place]
    yc_ref[features:, :] = jnp.ones((yc_ref.shape[0] - features, wide), BF16)
    points = yc_ref[:features, :].astype(F32)
    sq_ref[...] = SQUARE * fold(points * points)
    mj_ref[...] = jnp.full(mj_ref.shape, LOW, F32)
    lj_ref[...] = jnp.zeros(lj_ref.shape, F32)
    br = s_ref.shape[0]
    pieces = cols // 128

    def block(bi, _):
        rows = pl.ds(pl.multiple_of(bi * br, br), br)
        xb = xt_ref[rows, :]

        def scores(ci, high):
            cs = pl.ds(pl.multiple_of(ci * cols, cols), cols)
            s = jnp.dot(xb, yc_ref[:features, cs], preferred_element_type=F32) * CROSS - sq_ref[:, cs]
            s_ref[:, cs] = s
            for u in range(pieces):
                high = jnp.maximum(high, s[:, u * 128 : (u + 1) * 128])
            return high

        high = lax.fori_loop(0, wide // cols, scores, jnp.full((br, 128), LOW, F32))
        high = jnp.max(high, axis=1, keepdims=True)

        def sums(ci, acc):
            for u in range(pieces):
                cs = pl.ds(pl.multiple_of(ci * cols + u * 128, 128), 128)
                acc = acc + jnp.exp2(s_ref[:, cs] - high)
            return acc

        acc = lax.fori_loop(0, wide // cols, sums, jnp.zeros((br, 128), F32))
        r = -(high + jnp.log2(jnp.sum(acc, axis=1, keepdims=True)))
        r_ref[rows, :] = r

        def columns(ci, _):
            for u in range(pieces):
                cs = pl.ds(pl.multiple_of(ci * cols + u * 128, 128), 128)
                v = (s_ref[:, cs] + r).reshape(br // 8, 8, 128)
                old = mj_ref[:, cs]
                new = jnp.maximum(old, jnp.max(v, axis=0))
                lj_ref[:, cs] = lj_ref[:, cs] * jnp.exp2(old - new) + jnp.sum(jnp.exp2(v - new[None]), axis=0)
                mj_ref[:, cs] = new
            return 0

        lax.fori_loop(0, wide // cols, columns, 0)
        return 0

    lax.fori_loop(0, r_ref.shape[0] // br, block, 0)
    m = mj_ref[...]
    top = jnp.max(m, axis=0, keepdims=True)
    lse_ref[...] = top + jnp.log2(fold(lj_ref[...] * jnp.exp2(m - top)))


def plan_kernel(count, shift, br, cols, *refs):
    parts, (xt_ref, yc_ref, sq_ref, r_ref, p_ref, a_ref, s_ref, acc_ref, bias_ref) = refs[:count], refs[count:]
    top = functools.reduce(jnp.maximum, [q[...] for q in parts])
    lse = top + jnp.log2(sum(jnp.exp2(q[...] - top) for q in parts))
    bias_ref[...] = shift - lse - sq_ref[...]
    wide = bias_ref.shape[1]
    features = xt_ref.shape[1]
    acc_ref[...] = jnp.zeros(acc_ref.shape, F32)
    ones = jnp.ones((8, wide), BF16)

    def block(bi, _):
        rows = pl.ds(pl.multiple_of(bi * br, br), br)
        xb = xt_ref[rows, :]
        r = r_ref[rows, :]

        def chunk(ci, _):
            cs = pl.ds(pl.multiple_of(ci * cols, cols), cols)
            s = jnp.dot(xb, yc_ref[:features, cs], preferred_element_type=F32) * CROSS + bias_ref[:, cs] + r
            p_ref[rows, cs] = jnp.exp2(s).astype(BF16)
            return 0

        lax.fori_loop(0, wide // cols, chunk, 0)
        tile = p_ref[rows, :]
        t = lax.dot_general(ones, tile, NT, preferred_element_type=F32)[:1]
        a = 1.0 / t
        a_ref[:, rows] = a
        acc_ref[...] += jnp.dot(split3(a), tile, preferred_element_type=F32)
        return 0

    lax.fori_loop(0, p_ref.shape[0] // br, block, 0)
    s_ref[...] = fold(acc_ref[...])


def sweep(p_ref, w, br, step, acc_ref):
    w3 = split3(w)
    acc_ref[...] = jnp.zeros(acc_ref.shape, F32)

    def block(bi, _):
        rows = pl.ds(pl.multiple_of(bi * br, br), br)
        tile = p_ref[rows, :]
        q = fold(lax.dot_general(w3, tile, NT, preferred_element_type=F32))
        y = step(rows, q)
        acc_ref[...] += jnp.dot(split3(y), tile, preferred_element_type=F32)
        return 0

    lax.fori_loop(0, p_ref.shape[0] // br, block, 0)
    return fold(acc_ref[...])


def rhs_kernel(count, ratio, br, *refs):
    parts, (p_ref, gf_ref, g_ref, b_ref, cm_ref, m_ref, out_ref, acc_ref) = refs[:count], refs[count:]
    s = sum(q[...] for q in parts)
    b = ratio / s
    b_ref[...] = b
    cm_ref[...] = b * s

    def step(rows, q):
        m_ref[:, rows] = q
        return gf_ref[:, rows] / q

    out_ref[...] = g_ref[...] - b * sweep(p_ref, b, br, step, acc_ref)


def advance(parts, b, cm, dual, residual, direction):
    image = (1.0 + TAU) * cm * direction - b * sum(q[...] for q in parts)
    alpha = total(residual * residual) / total(direction * image)
    return alpha, dual + alpha * direction, residual - alpha * image


def cg_kernel(count, first, br, *refs):
    parts, refs = refs[:count], refs[count:]
    p_ref, a_ref, m_ref, b_ref, cm_ref = refs[:5]
    b = b_ref[...]
    if first:
        out = refs[5:]
        direction = sum(q[...] for q in parts)
        residual = direction
        dual = jnp.zeros_like(direction)
        mix = jnp.zeros(a_ref.shape, F32)
    else:
        dual_ref, res_ref, dir_ref, q_ref, mix_ref = refs[5:10]
        out = refs[10:]
        old = res_ref[...]
        before = dir_ref[...]
        alpha, dual, residual = advance(parts, b, cm_ref[...], dual_ref[...], old, before)
        direction = residual + total(residual * residual) / total(old * old) * before
        mix = mix_ref[...] + alpha * q_ref[...]
    dual_out, res_out, dir_out, q_out, mix_out, u_out, acc_ref = out
    dual_out[...] = dual
    res_out[...] = residual
    dir_out[...] = direction
    mix_out[...] = mix

    def step(rows, q):
        q_out[:, rows] = q
        return a_ref[:, rows] * q / m_ref[:, rows]

    u_out[...] = sweep(p_ref, b * direction, br, step, acc_ref)


def grad_kernel(count, group, br, *refs):
    parts, refs = refs[:count], refs[count:]
    me_ref, p_ref, a_ref, m_ref, b_ref, cm_ref, dual_ref, res_ref, dir_ref, q_ref, mix_ref = refs[:11]
    gf_ref, x_ref, yc_ref, src_ref, tgt_ref, w1_ref, w2_ref, ad_ref, dd_ref = refs[11:]
    me = me_ref[0]
    replicas, features, ns = x_ref.shape
    nt = tgt_ref.shape[2]
    b = b_ref[...]
    alpha, dual, _ = advance(parts, b, cm_ref[...], dual_ref[...], res_ref[...], dir_ref[...])
    a = a_ref[...]
    m = m_ref[...]
    mix = mix_ref[...] + alpha * q_ref[...]
    ad_ref[...] = down(a)
    dd_ref[...] = down((gf_ref[...] / a - mix) / m)
    wide = b.shape[1]
    for u in range(wide // 128):
        cs = slice(u * 128, (u + 1) * 128)
        plan = p_ref[:ns, cs].astype(F32) * (ad_ref[:ns, :] * b[:, cs])
        w1_ref[:, cs] = (plan * (dd_ref[:ns, :] + dual[:, cs])).astype(BF16)
    out = lax.dot_general(yc_ref[...], w1_ref[...], NT, preferred_element_type=F32)
    src_ref[...] = 2.0 * (x_ref[0].astype(F32) * out[features : features + 1] - out[:features])

    base = (me // group) * (group * nt)
    q_ref_b = b_ref
    half = group * nt
    dual_mine = pick(dual, me // group, half)
    for u in range(half // 128):
        cs = slice(u * 128, (u + 1) * 128)
        cd = pl.ds(pl.multiple_of(base + u * 128, 128), 128)
        bb = q_ref_b[:, cd]
        plan = p_ref[:, cd].astype(F32) * (ad_ref[...] * bb)
        w2_ref[:, cs] = (plan * (dd_ref[...] + dual_mine[:, cs])).astype(BF16)
    pulled = jnp.zeros((features, half), F32)
    for k in range(replicas):
        pulled = pulled + jnp.dot(x_ref[k], w2_ref[k * ns : (k + 1) * ns, :], preferred_element_type=F32)
    cols_w = jnp.dot(jnp.ones((8, w2_ref.shape[0]), BF16), w2_ref[...], preferred_element_type=F32)[:1]
    mine = yc_ref[:features, pl.ds(pl.multiple_of(base, 128), half)].astype(F32)
    part = 2.0 * (mine * cols_w - pulled)
    for k in range(group):
        tgt_ref[jnp.bitwise_xor(k, me % group)] = part[:, k * nt : (k + 1) * nt]


def pick(vector, index, size):
    out = vector[:, :size]
    for k in range(1, vector.shape[1] // size):
        out = jnp.where(index == k, vector[:, k * size : (k + 1) * size], out)
    return out


def call(kernel, operands, outs, scratch, smem=()):
    return pl.pallas_call(
        kernel,
        out_shape=outs,
        in_specs=[SMEM if i in smem else VMEM for i in range(len(operands))],
        out_specs=[VMEM] * len(outs),
        scratch_shapes=scratch,
        compiler_params=pltpu.CompilerParams(vmem_limit_bytes=60 * 1024 * 1024),
    )(*operands)


def body(src_points, tgt_points, grad_f, grad_g):
    rows_axis, cols_axis = lax.axis_size("row"), lax.axis_size("col")
    devices = rows_axis * cols_axis
    group = 2 * cols_axis
    replicas = devices // group
    features, ns = src_points.shape
    nt = tgt_points.shape[1]
    wide = devices * nt
    rows = replicas * ns
    row, col = lax.axis_index("row"), lax.axis_index("col")
    me = row * cols_axis + col
    me_ref = me.astype(jnp.int32).reshape(1)

    def swap(value, mask):
        return lax.ppermute(value, AXES, [(i, i ^ mask) for i in range(devices)])

    bits = [1 << i for i in range(1, group.bit_length() - 1)]
    stages = [[1]]
    for i in range(0, len(bits), 2):
        pair = bits[i : i + 2]
        stages.append(pair + ([pair[0] | pair[1]] if len(pair) == 2 else []))

    def exchange(value, combine):
        for stage in stages[:-1]:
            value = combine([value] + [swap(value, mask) for mask in stage])
        return [value] + [swap(value, mask) for mask in stages[-1]]

    x = src_points[None]
    y = tgt_points[None]
    gf = lax.dynamic_slice(grad_f, (col * ns,), (ns,))[None]
    mask = group
    while mask < devices:
        x = jnp.concatenate([x, swap(x, mask)])
        y = jnp.concatenate([y, swap(y, mask)])
        gf = jnp.concatenate([gf, swap(gf, mask)])
        mask *= 2
    for stage in stages[1:] + stages[:1]:
        y = jnp.concatenate([y] + [swap(y, mask) for mask in stage])
    gf = gf.reshape(1, rows)
    own = (jnp.arange(cols_axis)[None, :, None] == col) & (row % 2 == 0)
    g = jnp.where(own, grad_g.reshape(rows_axis, 1, nt), 0.0).reshape(1, wide)

    br = min(128, rows)
    cols = min(1024, wide)
    vec = jax.ShapeDtypeStruct((1, wide), F32)
    line = jax.ShapeDtypeStruct((1, rows), F32)
    acc = pltpu.VMEM((8, wide), F32)
    extended = features + 16
    xt, yc, sq, r, lse = call(
        functools.partial(lse_kernel, group, cols),
        (me_ref, x, y),
        (
            jax.ShapeDtypeStruct((rows, features), BF16),
            jax.ShapeDtypeStruct((extended, wide), BF16),
            vec,
            jax.ShapeDtypeStruct((rows, 1), F32),
            vec,
        ),
        [pltpu.VMEM((br, wide), F32), acc, acc],
        smem=(0,),
    )

    def join(values):
        top = functools.reduce(jnp.maximum, values)
        return top + jnp.log2(sum(jnp.exp2(v - top) for v in values))

    parts = exchange(lse, join)
    count = len(parts)
    wb = min(256, rows)
    p, a, s = call(
        functools.partial(plan_kernel, count, math.log2(ns / nt), wb, cols),
        (*parts, xt, yc, sq, r),
        (jax.ShapeDtypeStruct((rows, wide), BF16), line, vec),
        [acc, pltpu.VMEM((1, wide), F32)],
    )
    parts = exchange(s, sum)
    b, cm, m, u = call(
        functools.partial(rhs_kernel, count, ns / nt, wb),
        (*parts, p, gf, g),
        (vec, vec, line, vec),
        [acc],
    )
    state = ()
    for step in range(CG):
        parts = exchange(u, sum)
        *state, u = call(
            functools.partial(cg_kernel, count, step == 0, wb),
            (*parts, p, a, m, b, cm, *state),
            (vec, vec, vec, line, line, vec),
            [acc],
        )
    parts = exchange(u, sum)
    grad_src, part = call(
        functools.partial(grad_kernel, count, group, wb),
        (*parts, me_ref, p, a, m, b, cm, *state, gf, x, yc),
        (jax.ShapeDtypeStruct((features, ns), F32), jax.ShapeDtypeStruct((group, features, nt), F32)),
        [
            pltpu.VMEM((ns, wide), BF16),
            pltpu.VMEM((rows, group * nt), BF16),
            pltpu.VMEM((rows, 128), F32),
            pltpu.VMEM((rows, 128), F32),
        ],
        smem=(count,),
    )
    for stage in stages:
        size = len(stage) + 1
        unit = stage[0]
        part = part.reshape(part.shape[0] // size, size, features, nt)
        part = sum([swap(part[:, mask // unit], mask) for mask in stage], part[:, 0])
    return grad_src, part.reshape(features, nt)


def solution(mesh):
    in_specs = (P(None, ("row", "col")), P(None, ("col", "row")), P("row"), P("col"))
    out_specs = (P(None, ("row", "col")), P(None, ("col", "row")))
    return jax.shard_map(body, mesh=mesh, in_specs=in_specs, out_specs=out_specs, check_vma=False)
```

```python
import functools
import math

import jax
import jax.numpy as jnp
from jax import lax
from jax.experimental import pallas as pl
from jax.experimental.pallas import tpu as pltpu
from jax.sharding import PartitionSpec as P

CG = 3
EPS = 4.0
TAU = 0.1
AXES = ("row", "col")
LOW = -3.0e38
LOG2E = math.log2(math.e)
CROSS = 2.0 * LOG2E / EPS
SQUARE = LOG2E / EPS
F32 = jnp.float32
BF16 = jnp.bfloat16
NT = (((1,), (1,)), ((), ()))
VMEM = pl.BlockSpec(memory_space=pltpu.VMEM)
SMEM = pl.BlockSpec(memory_space=pltpu.SMEM)


def split3(vector):
    high = vector.astype(BF16).astype(F32)
    rest = vector - high
    mid = rest.astype(BF16).astype(F32)
    low = rest - mid
    shape = (8, vector.shape[1])
    line = lax.broadcasted_iota(jnp.int32, shape, 0)
    zero = jnp.zeros(shape, F32)
    rows = jnp.where(line == 0, high, jnp.where(line == 1, mid, jnp.where(line == 2, low, zero)))
    return rows.astype(BF16)


def total(vector):
    return jnp.sum(vector, axis=1, keepdims=True)


def fold(rows):
    return jnp.sum(rows, axis=0, keepdims=True)


def down(vector):
    return jnp.broadcast_to(vector, (128, vector.shape[1])).T


def lse_kernel(group, cols, me_ref, x_ref, y_ref, xt_ref, yc_ref, sq_ref, r_ref, lse_ref, s_ref, mj_ref, lj_ref):
    me = me_ref[0]
    replicas, features, ns = x_ref.shape
    devices, _, nt = y_ref.shape
    wide = devices * nt
    for k in range(replicas):
        xt_ref[k * ns : (k + 1) * ns, :] = x_ref[k].T
    for t in range(devices):
        k = jnp.bitwise_xor(t, me)
        inner = k % group
        place = (inner % 2) * (devices // 2) + (inner // 2) * replicas + k // group
        yc_ref[:features, t * nt : (t + 1) * nt] = y_ref[place]
    yc_ref[features:, :] = jnp.ones((yc_ref.shape[0] - features, wide), BF16)
    points = yc_ref[:features, :].astype(F32)
    sq_ref[...] = SQUARE * fold(points * points)
    mj_ref[...] = jnp.full(mj_ref.shape, LOW, F32)
    lj_ref[...] = jnp.zeros(lj_ref.shape, F32)
    br = s_ref.shape[0]
    pieces = cols // 128

    def block(bi, _):
        rows = pl.ds(pl.multiple_of(bi * br, br), br)
        xb = xt_ref[rows, :]

        def scores(ci, high):
            cs = pl.ds(pl.multiple_of(ci * cols, cols), cols)
            s = jnp.dot(xb, yc_ref[:features, cs], preferred_element_type=F32) * CROSS - sq_ref[:, cs]
            s_ref[:, cs] = s
            for u in range(pieces):
                high = jnp.maximum(high, s[:, u * 128 : (u + 1) * 128])
            return high

        high = lax.fori_loop(0, wide // cols, scores, jnp.full((br, 128), LOW, F32))
        high = jnp.max(high, axis=1, keepdims=True)

        def sums(ci, acc):
            for u in range(pieces):
                cs = pl.ds(pl.multiple_of(ci * cols + u * 128, 128), 128)
                acc = acc + jnp.exp2(s_ref[:, cs] - high)
            return acc

        acc = lax.fori_loop(0, wide // cols, sums, jnp.zeros((br, 128), F32))
        r = -(high + jnp.log2(jnp.sum(acc, axis=1, keepdims=True)))
        r_ref[rows, :] = r

        def columns(ci, _):
            for u in range(pieces):
                cs = pl.ds(pl.multiple_of(ci * cols + u * 128, 128), 128)
                v = (s_ref[:, cs] + r).reshape(br // 8, 8, 128)
                old = mj_ref[:, cs]
                new = jnp.maximum(old, jnp.max(v, axis=0))
                lj_ref[:, cs] = lj_ref[:, cs] * jnp.exp2(old - new) + jnp.sum(jnp.exp2(v - new[None]), axis=0)
                mj_ref[:, cs] = new
            return 0

        lax.fori_loop(0, wide // cols, columns, 0)
        return 0

    lax.fori_loop(0, r_ref.shape[0] // br, block, 0)
    m = mj_ref[...]
    top = jnp.max(m, axis=0, keepdims=True)
    lse_ref[...] = top + jnp.log2(fold(lj_ref[...] * jnp.exp2(m - top)))


def plan_kernel(count, shift, br, cols, *refs):
    parts, (xt_ref, yc_ref, sq_ref, r_ref, p_ref, a_ref, s_ref, bias_ref) = refs[:count], refs[count:]
    top = functools.reduce(jnp.maximum, [q[...] for q in parts])
    lse = top + jnp.log2(sum(jnp.exp2(q[...] - top) for q in parts))
    bias_ref[...] = shift - lse - sq_ref[...]
    wide = bias_ref.shape[1]
    features = xt_ref.shape[1]

    def block(bi, _):
        rows = pl.ds(pl.multiple_of(bi * br, br), br)
        xb = xt_ref[rows, :]
        r = r_ref[rows, :]

        def chunk(ci, _):
            cs = pl.ds(pl.multiple_of(ci * cols, cols), cols)
            s = jnp.dot(xb, yc_ref[:features, cs], preferred_element_type=F32) * CROSS + bias_ref[:, cs] + r
            p_ref[rows, cs] = jnp.exp2(s).astype(BF16)
            return 0

        lax.fori_loop(0, wide // cols, chunk, 0)
        return 0

    lax.fori_loop(0, p_ref.shape[0] // br, block, 0)

    def step(t):
        a = 1.0 / t
        a_ref[...] = a
        return a

    s_ref[...] = sweep(p_ref, jnp.ones((1, wide), F32), step)


def sweep(p_ref, w, step):
    tile = p_ref[...]
    q = fold(lax.dot_general(split3(w), tile, NT, preferred_element_type=F32))
    return fold(jnp.dot(split3(step(q)), tile, preferred_element_type=F32))


def rhs_kernel(count, ratio, *refs):
    parts, (p_ref, gf_ref, g_ref, b_ref, cm_ref, m_ref, out_ref) = refs[:count], refs[count:]
    s = sum(q[...] for q in parts)
    b = ratio / s
    b_ref[...] = b
    cm_ref[...] = b * s

    def step(q):
        m_ref[...] = q
        return gf_ref[...] / q

    out_ref[...] = g_ref[...] - b * sweep(p_ref, b, step)


def advance(parts, b, cm, dual, residual, direction):
    image = (1.0 + TAU) * cm * direction - b * sum(q[...] for q in parts)
    alpha = total(residual * residual) / total(direction * image)
    return alpha, dual + alpha * direction, residual - alpha * image


def cg_kernel(count, first, *refs):
    parts, refs = refs[:count], refs[count:]
    p_ref, a_ref, m_ref, b_ref, cm_ref = refs[:5]
    b = b_ref[...]
    if first:
        out = refs[5:]
        direction = sum(q[...] for q in parts)
        residual = direction
        dual = jnp.zeros_like(direction)
        mix = jnp.zeros(a_ref.shape, F32)
    else:
        dual_ref, res_ref, dir_ref, q_ref, mix_ref = refs[5:10]
        out = refs[10:]
        old = res_ref[...]
        before = dir_ref[...]
        alpha, dual, residual = advance(parts, b, cm_ref[...], dual_ref[...], old, before)
        direction = residual + total(residual * residual) / total(old * old) * before
        mix = mix_ref[...] + alpha * q_ref[...]
    dual_out, res_out, dir_out, q_out, mix_out, u_out = out
    dual_out[...] = dual
    res_out[...] = residual
    dir_out[...] = direction
    mix_out[...] = mix

    def step(q):
        q_out[...] = q
        return a_ref[...] * q / m_ref[...]

    u_out[...] = sweep(p_ref, b * direction, step)


def grad_kernel(count, group, *refs):
    parts, refs = refs[:count], refs[count:]
    me_ref, p_ref, a_ref, m_ref, b_ref, cm_ref, dual_ref, res_ref, dir_ref, q_ref, mix_ref = refs[:11]
    gf_ref, x_ref, yc_ref, src_ref, tgt_ref, w1_ref, w2_ref, ad_ref, dd_ref = refs[11:]
    me = me_ref[0]
    replicas, features, ns = x_ref.shape
    nt = tgt_ref.shape[2]
    b = b_ref[...]
    alpha, dual, _ = advance(parts, b, cm_ref[...], dual_ref[...], res_ref[...], dir_ref[...])
    a = a_ref[...]
    m = m_ref[...]
    mix = mix_ref[...] + alpha * q_ref[...]
    ad_ref[...] = down(a)
    dd_ref[...] = down((gf_ref[...] / a - mix) / m)
    wide = b.shape[1]
    for u in range(wide // 128):
        cs = slice(u * 128, (u + 1) * 128)
        plan = p_ref[:ns, cs].astype(F32) * (ad_ref[:ns, :] * b[:, cs])
        w1_ref[:, cs] = (plan * (dd_ref[:ns, :] + dual[:, cs])).astype(BF16)
    out = lax.dot_general(yc_ref[...], w1_ref[...], NT, preferred_element_type=F32)
    src_ref[...] = 2.0 * (x_ref[0].astype(F32) * out[features : features + 1] - out[:features])

    base = (me // group) * (group * nt)
    q_ref_b = b_ref
    half = group * nt
    dual_mine = pick(dual, me // group, half)
    for u in range(half // 128):
        cs = slice(u * 128, (u + 1) * 128)
        cd = pl.ds(pl.multiple_of(base + u * 128, 128), 128)
        bb = q_ref_b[:, cd]
        plan = p_ref[:, cd].astype(F32) * (ad_ref[...] * bb)
        w2_ref[:, cs] = (plan * (dd_ref[...] + dual_mine[:, cs])).astype(BF16)
    pulled = jnp.zeros((features, half), F32)
    for k in range(replicas):
        pulled = pulled + jnp.dot(x_ref[k], w2_ref[k * ns : (k + 1) * ns, :], preferred_element_type=F32)
    cols_w = jnp.dot(jnp.ones((8, w2_ref.shape[0]), BF16), w2_ref[...], preferred_element_type=F32)[:1]
    mine = yc_ref[:features, pl.ds(pl.multiple_of(base, 128), half)].astype(F32)
    part = 2.0 * (mine * cols_w - pulled)
    for k in range(group):
        tgt_ref[jnp.bitwise_xor(k, me % group)] = part[:, k * nt : (k + 1) * nt]


def pick(vector, index, size):
    out = vector[:, :size]
    for k in range(1, vector.shape[1] // size):
        out = jnp.where(index == k, vector[:, k * size : (k + 1) * size], out)
    return out


def call(kernel, operands, outs, scratch, smem=()):
    return pl.pallas_call(
        kernel,
        out_shape=outs,
        in_specs=[SMEM if i in smem else VMEM for i in range(len(operands))],
        out_specs=[VMEM] * len(outs),
        scratch_shapes=scratch,
        compiler_params=pltpu.CompilerParams(vmem_limit_bytes=24 * 1024 * 1024),
    )(*operands)


def body(src_points, tgt_points, grad_f, grad_g):
    rows_axis, cols_axis = lax.axis_size("row"), lax.axis_size("col")
    devices = rows_axis * cols_axis
    group = 2 * cols_axis
    replicas = devices // group
    features, ns = src_points.shape
    nt = tgt_points.shape[1]
    wide = devices * nt
    rows = replicas * ns
    row, col = lax.axis_index("row"), lax.axis_index("col")
    me = row * cols_axis + col
    me_ref = me.astype(jnp.int32).reshape(1)

    def swap(value, mask):
        return lax.ppermute(value, AXES, [(i, i ^ mask) for i in range(devices)])

    bits = [1 << i for i in range(1, group.bit_length() - 1)]
    stages = [[1]]
    for i in range(0, len(bits), 2):
        pair = bits[i : i + 2]
        stages.append(pair + ([pair[0] | pair[1]] if len(pair) == 2 else []))

    def exchange(value, combine):
        for stage in stages[:-1]:
            value = combine([value] + [swap(value, mask) for mask in stage])
        return [value] + [swap(value, mask) for mask in stages[-1]]

    x = src_points[None]
    y = tgt_points[None]
    gf = lax.dynamic_slice(grad_f, (col * ns,), (ns,))[None]
    mask = group
    while mask < devices:
        x = jnp.concatenate([x, swap(x, mask)])
        y = jnp.concatenate([y, swap(y, mask)])
        gf = jnp.concatenate([gf, swap(gf, mask)])
        mask *= 2
    for stage in stages[1:] + stages[:1]:
        y = jnp.concatenate([y] + [swap(y, mask) for mask in stage])
    gf = gf.reshape(1, rows)
    own = (jnp.arange(cols_axis)[None, :, None] == col) & (row % 2 == 0)
    g = jnp.where(own, grad_g.reshape(rows_axis, 1, nt), 0.0).reshape(1, wide)

    br = min(128, rows)
    cols = min(1024, wide)
    vec = jax.ShapeDtypeStruct((1, wide), F32)
    line = jax.ShapeDtypeStruct((1, rows), F32)
    acc = pltpu.VMEM((8, wide), F32)
    extended = features + 16
    xt, yc, sq, r, lse = call(
        functools.partial(lse_kernel, group, cols),
        (me_ref, x, y),
        (
            jax.ShapeDtypeStruct((rows, features), BF16),
            jax.ShapeDtypeStruct((extended, wide), BF16),
            vec,
            jax.ShapeDtypeStruct((rows, 1), F32),
            vec,
        ),
        [pltpu.VMEM((br, wide), F32), acc, acc],
        smem=(0,),
    )

    def join(values):
        top = functools.reduce(jnp.maximum, values)
        return top + jnp.log2(sum(jnp.exp2(v - top) for v in values))

    parts = exchange(lse, join)
    count = len(parts)
    wb = min(256, rows)
    p, a, s = call(
        functools.partial(plan_kernel, count, math.log2(ns / nt), wb, cols),
        (*parts, xt, yc, sq, r),
        (jax.ShapeDtypeStruct((rows, wide), BF16), line, vec),
        [pltpu.VMEM((1, wide), F32)],
    )
    parts = exchange(s, sum)
    b, cm, m, u = call(
        functools.partial(rhs_kernel, count, ns / nt),
        (*parts, p, gf, g),
        (vec, vec, line, vec),
        [],
    )
    state = ()
    for step in range(CG):
        parts = exchange(u, sum)
        *state, u = call(
            functools.partial(cg_kernel, count, step == 0),
            (*parts, p, a, m, b, cm, *state),
            (vec, vec, vec, line, line, vec),
            [],
        )
    parts = exchange(u, sum)
    grad_src, part = call(
        functools.partial(grad_kernel, count, group),
        (*parts, me_ref, p, a, m, b, cm, *state, gf, x, yc),
        (jax.ShapeDtypeStruct((features, ns), F32), jax.ShapeDtypeStruct((group, features, nt), F32)),
        [
            pltpu.VMEM((ns, wide), BF16),
            pltpu.VMEM((rows, group * nt), BF16),
            pltpu.VMEM((rows, 128), F32),
            pltpu.VMEM((rows, 128), F32),
        ],
        smem=(count,),
    )
    for stage in stages:
        size = len(stage) + 1
        unit = stage[0]
        part = part.reshape(part.shape[0] // size, size, features, nt)
        part = sum([swap(part[:, mask // unit], mask) for mask in stage], part[:, 0])
    return grad_src, part.reshape(features, nt)


def solution(mesh):
    in_specs = (P(None, ("row", "col")), P(None, ("col", "row")), P("row"), P("col"))
    out_specs = (P(None, ("row", "col")), P(None, ("col", "row")))
    return jax.shard_map(body, mesh=mesh, in_specs=in_specs, out_specs=out_specs, check_vma=False)
```

```python
import functools
import math

import jax
import jax.numpy as jnp
from jax import lax
from jax.experimental import pallas as pl
from jax.experimental.pallas import tpu as pltpu
from jax.sharding import PartitionSpec as P

CG = 3
EPS = 4.0
TAU = 0.1
AXES = ("row", "col")
LOW = -3.0e38
TINY = 2.0**-80
LIMIT = 80.0
SPAN = 4096
ELEMENTS = 4 * 1024 * 1024
LOG2E = math.log2(math.e)
CROSS = 2.0 * LOG2E / EPS
SQUARE = LOG2E / EPS
F32 = jnp.float32
BF16 = jnp.bfloat16
NT = (((1,), (1,)), ((), ()))
VMEM = pl.BlockSpec(memory_space=pltpu.VMEM)
SMEM = pl.BlockSpec(memory_space=pltpu.SMEM)


def split3(vector):
    high = vector.astype(BF16).astype(F32)
    rest = vector - high
    mid = rest.astype(BF16).astype(F32)
    low = rest - mid
    shape = (8, vector.shape[1])
    line = lax.broadcasted_iota(jnp.int32, shape, 0)
    zero = jnp.zeros(shape, F32)
    rows = jnp.where(line == 0, high, jnp.where(line == 1, mid, jnp.where(line == 2, low, zero)))
    return rows.astype(BF16)


def total(vector):
    return jnp.sum(vector, axis=1, keepdims=True)


def fold(rows):
    return jnp.sum(rows, axis=0, keepdims=True)


def down(vector):
    return jnp.broadcast_to(vector, (128, vector.shape[1])).T


def over(wide, step, carry):
    span = min(wide, SPAN)
    if wide == span:
        return step(0, carry)
    return lax.fori_loop(0, wide // span, lambda i, c: step(pl.multiple_of(i * span, span), c), carry)


def lanes(base, offset, size):
    return pl.ds(pl.multiple_of(base + offset, 128), size) if not isinstance(base, int) else pl.ds(base + offset, size)


def lse_kernel(
    group, br, me_ref, x_ref, y_ref, lhs_ref, rhs_ref, yc_ref, p_ref, r_ref, lse_ref, sa_ref, sb_ref, acc_ref, m_ref
):
    me = me_ref[0]
    replicas, features, ns = x_ref.shape
    devices, _, nt = y_ref.shape
    rows, wide = p_ref.shape
    extra = lhs_ref.shape[1] - 3 * features
    lhs_ref[:, 3 * features :] = jnp.ones((rows, extra), BF16)
    for k in range(replicas):
        points = x_ref[k].T
        for c in range(3):
            lhs_ref[k * ns : (k + 1) * ns, c * features : (c + 1) * features] = points
    yc_ref[features:, :] = jnp.ones((yc_ref.shape[0] - features, wide), BF16)
    for t in range(devices):
        cs = slice(t * nt, (t + 1) * nt)
        k = jnp.bitwise_xor(t, me)
        inner = k % group
        points = y_ref[(inner % 2) * (devices // 2) + (inner // 2) * replicas + k // group]
        yc_ref[:features, cs] = points
        points = points.astype(F32)
        square = fold(points * points) * -SQUARE
        value = points * CROSS
        high = value.astype(BF16)
        rest = value - high.astype(F32)
        mid = rest.astype(BF16)
        rhs_ref[:features, cs] = high
        rhs_ref[features : 2 * features, cs] = mid
        rhs_ref[2 * features : 3 * features, cs] = (rest - mid.astype(F32)).astype(BF16)
        rhs_ref[3 * features : 3 * features + 8, cs] = split3(square)
        rhs_ref[3 * features + 8 :, cs] = jnp.zeros((extra - 8, nt), BF16)
    scratch = (sa_ref, sb_ref)

    def scores(b):
        lb = lhs_ref[b * br : (b + 1) * br, :]
        s_ref = scratch[b % 2]

        def step(base, high):
            for u in range(0, min(wide, SPAN), 256):
                cs = lanes(base, u, 256)
                s = jnp.dot(lb, rhs_ref[:, cs], preferred_element_type=F32)
                s_ref[:, cs] = s
                high = jnp.maximum(high, jnp.maximum(s[:, :128], s[:, 128:]))
            return high

        return jnp.max(over(wide, step, jnp.full((br, 128), LOW, F32)), axis=1, keepdims=True)

    def exps(b, high):
        s_ref = scratch[b % 2]
        rs = slice(b * br, (b + 1) * br)
        hb = jnp.broadcast_to(high, (br, 128))

        def step(base, acc):
            for u in range(0, min(wide, SPAN), 128):
                cs = lanes(base, u, 128)
                e = jnp.exp2(s_ref[:, cs] - hb)
                p_ref[rs, cs] = e.astype(BF16)
                acc = acc + e
            return acc

        sums = jnp.sum(over(wide, step, jnp.zeros((br, 128), F32)), axis=1, keepdims=True)
        r_ref[rs, :] = jnp.broadcast_to(-(high + jnp.log2(sums)), (br, 128))
        return jnp.broadcast_to(1.0 / sums, (br, 128)).T[:1]

    count = rows // br
    inverse = []
    high = scores(0)
    for b in range(count):
        after = scores(b + 1) if b + 1 < count else None
        inverse.append(exps(b, high))
        high = after
    s = pulled(p_ref, jnp.concatenate(inverse, axis=1))
    lse_ref[...] = jnp.log2(jnp.maximum(s, TINY))

    @pl.when(jnp.min(s) < TINY)
    def _():
        acc_ref[...] = jnp.zeros(acc_ref.shape, F32)
        m_ref[...] = jnp.full(m_ref.shape, LOW, F32)

        def step(i, _):
            rs, cs, v = tile_scores(i, lhs_ref, rhs_ref, r_ref)
            v = v.reshape(v.shape[0] // 8, 8, 128)
            old = m_ref[:, cs]
            new = jnp.maximum(old, jnp.max(v, axis=0))
            acc_ref[:, cs] = acc_ref[:, cs] * jnp.exp2(old - new) + fold3(jnp.exp2(v - new[None]))
            m_ref[:, cs] = new
            return 0

        lax.fori_loop(0, (rows // 128) * (wide // 128), step, 0)
        m = m_ref[...]
        top = jnp.max(m, axis=0, keepdims=True)
        lse_ref[...] = top + jnp.log2(fold(acc_ref[...] * jnp.exp2(m - top)))


def fold3(values):
    return jnp.sum(values, axis=0)


def tile_scores(i, lhs_ref, rhs_ref, r_ref):
    across = rhs_ref.shape[1] // 128
    rs = pl.ds(pl.multiple_of(i // across * 128, 128), 128)
    cs = pl.ds(pl.multiple_of(i % across * 128, 128), 128)
    return rs, cs, jnp.dot(lhs_ref[rs, :], rhs_ref[:, cs], preferred_element_type=F32) + r_ref[rs, :]


def pushed(p_ref, w):
    return fold(lax.dot_general(split3(w), p_ref[...], NT, preferred_element_type=F32))


def pulled(p_ref, y):
    return fold(jnp.dot(split3(y), p_ref[...], preferred_element_type=F32))


def plan_kernel(count, shift, *refs):
    parts, (lhs_ref, rhs_ref, r_ref, old_ref, p_ref, scale_ref, a_ref, s_ref) = refs[:count], refs[count:]
    top = functools.reduce(jnp.maximum, [q[...] for q in parts])
    c = shift - top - jnp.log2(sum(jnp.exp2(q[...] - top) for q in parts))
    rows, wide = p_ref.shape
    plain = jnp.max(c) <= LIMIT
    scale_ref[...] = jnp.exp2(jnp.minimum(c, LIMIT))

    @pl.when(jnp.logical_not(plain))
    def _():
        scale_ref[...] = c

        def step(i, _):
            rs, cs, v = tile_scores(i, lhs_ref, rhs_ref, r_ref)
            p_ref[rs, cs] = jnp.exp2(v + scale_ref[:, cs]).astype(BF16)
            return 0

        lax.fori_loop(0, (rows // 128) * (wide // 128), step, 0)
        scale_ref[...] = jnp.ones((1, wide), F32)

    scale = scale_ref[...]
    a = 1.0 / pushed(p_ref, scale)
    a_ref[...] = a
    s_ref[...] = scale * pulled(p_ref, a)


def rhs_kernel(count, ratio, *refs):
    parts, (p_ref, scale_ref, gf_ref, g_ref, b_ref, cm_ref, m_ref, out_ref) = refs[:count], refs[count:]
    s = sum(q[...] for q in parts)
    b = ratio / s
    b_ref[...] = b
    cm_ref[...] = b * s

    scale = scale_ref[...]
    m = pushed(p_ref, scale * b)
    m_ref[...] = m
    out_ref[...] = g_ref[...] - b * scale * pulled(p_ref, gf_ref[...] / m)


def advance(parts, b, cm, dual, residual, direction):
    image = (1.0 + TAU) * cm * direction - b * sum(q[...] for q in parts)
    alpha = total(residual * residual) / total(direction * image)
    return alpha, dual + alpha * direction, residual - alpha * image


def cg_kernel(count, first, *refs):
    parts, refs = refs[:count], refs[count:]
    p_ref, scale_ref, a_ref, m_ref, b_ref, cm_ref = refs[:6]
    b = b_ref[...]
    if first:
        out = refs[6:]
        direction = sum(q[...] for q in parts)
        residual = direction
        dual = jnp.zeros_like(direction)
        mix = jnp.zeros(a_ref.shape, F32)
    else:
        dual_ref, res_ref, dir_ref, q_ref, mix_ref = refs[6:11]
        out = refs[11:]
        old = res_ref[...]
        before = dir_ref[...]
        alpha, dual, residual = advance(parts, b, cm_ref[...], dual_ref[...], old, before)
        direction = residual + total(residual * residual) / total(old * old) * before
        mix = mix_ref[...] + alpha * q_ref[...]
    dual_out, res_out, dir_out, q_out, mix_out, u_out = out
    dual_out[...] = dual
    res_out[...] = residual
    dir_out[...] = direction
    mix_out[...] = mix

    scale = scale_ref[...]
    q = pushed(p_ref, scale * b * direction)
    q_out[...] = q
    u_out[...] = scale * pulled(p_ref, a_ref[...] * q / m_ref[...])


def grad_kernel(count, group, *refs):
    parts, refs = refs[:count], refs[count:]
    me_ref, p_ref, scale_ref, a_ref, m_ref, b_ref, cm_ref, dual_ref, res_ref, dir_ref, q_ref, mix_ref = refs[:12]
    gf_ref, x_ref, yc_ref, src_ref, tgt_ref, w1_ref, w2_ref, ad_ref, dd_ref = refs[12:]
    me = me_ref[0]
    replicas, features, ns = x_ref.shape
    nt = tgt_ref.shape[2]
    b = b_ref[...]
    alpha, dual, _ = advance(parts, b, cm_ref[...], dual_ref[...], res_ref[...], dir_ref[...])
    a = a_ref[...]
    m = m_ref[...]
    mix = mix_ref[...] + alpha * q_ref[...]
    ad_ref[...] = down(a)
    dd_ref[...] = down((gf_ref[...] / a - mix) / m)
    wide = b.shape[1]
    b = b * scale_ref[...]
    for u in range(wide // 128):
        cs = slice(u * 128, (u + 1) * 128)
        plan = p_ref[:ns, cs].astype(F32) * (ad_ref[:ns, :] * b[:, cs])
        w1_ref[:, cs] = (plan * (dd_ref[:ns, :] + dual[:, cs])).astype(BF16)
    out = lax.dot_general(yc_ref[...], w1_ref[...], NT, preferred_element_type=F32)
    src_ref[...] = 2.0 * (x_ref[0].astype(F32) * out[features : features + 1] - out[:features])

    base = (me // group) * (group * nt)
    half = group * nt
    dual_mine = pick(dual, me // group, half)
    b_mine = pick(b, me // group, half)
    for u in range(half // 128):
        cs = slice(u * 128, (u + 1) * 128)
        cd = pl.ds(pl.multiple_of(base + u * 128, 128), 128)
        plan = p_ref[:, cd].astype(F32) * (ad_ref[...] * b_mine[:, cs])
        w2_ref[:, cs] = (plan * (dd_ref[...] + dual_mine[:, cs])).astype(BF16)
    pulled = jnp.zeros((features, half), F32)
    for k in range(replicas):
        pulled = pulled + jnp.dot(x_ref[k], w2_ref[k * ns : (k + 1) * ns, :], preferred_element_type=F32)
    cols_w = jnp.dot(jnp.ones((8, w2_ref.shape[0]), BF16), w2_ref[...], preferred_element_type=F32)[:1]
    mine = yc_ref[:features, pl.ds(pl.multiple_of(base, 128), half)].astype(F32)
    part = 2.0 * (mine * cols_w - pulled)
    for k in range(group):
        tgt_ref[jnp.bitwise_xor(k, me % group)] = part[:, k * nt : (k + 1) * nt]


def pick(vector, index, size):
    out = vector[:, :size]
    for k in range(1, vector.shape[1] // size):
        out = jnp.where(index == k, vector[:, k * size : (k + 1) * size], out)
    return out


def call(kernel, operands, outs, scratch, smem=(), limit=24, alias={}):
    return pl.pallas_call(
        kernel,
        out_shape=outs,
        in_specs=[SMEM if i in smem else VMEM for i in range(len(operands))],
        out_specs=[VMEM] * len(outs),
        scratch_shapes=scratch,
        input_output_aliases=alias,
        compiler_params=pltpu.CompilerParams(vmem_limit_bytes=limit * 1024 * 1024),
    )(*operands)


def body(src_points, tgt_points, grad_f, grad_g):
    rows_axis, cols_axis = lax.axis_size("row"), lax.axis_size("col")
    devices = rows_axis * cols_axis
    features, ns = src_points.shape
    nt = tgt_points.shape[1]
    wide = devices * nt
    group = 2
    while group < devices and devices // group * ns * wide > ELEMENTS:
        group *= 2
    replicas = devices // group
    rows = replicas * ns
    row, col = lax.axis_index("row"), lax.axis_index("col")
    me = row * cols_axis + col
    me_ref = me.astype(jnp.int32).reshape(1)

    def swap(value, mask):
        return lax.ppermute(value, AXES, [(i, i ^ mask) for i in range(devices)])

    bits = [1 << i for i in range(1, group.bit_length() - 1)]
    stages = [[1]]
    for i in range(0, len(bits), 2):
        pair = bits[i : i + 2]
        stages.append(pair + ([pair[0] | pair[1]] if len(pair) == 2 else []))

    def exchange(value, combine):
        for stage in stages[:-1]:
            value = combine([value] + [swap(value, mask) for mask in stage])
        return [value] + [swap(value, mask) for mask in stages[-1]]

    x = src_points[None]
    y = tgt_points[None]
    gf = lax.dynamic_slice(grad_f, (col * ns,), (ns,))[None]
    mask = group
    while mask < devices:
        x = jnp.concatenate([x, swap(x, mask)])
        y = jnp.concatenate([y, swap(y, mask)])
        gf = jnp.concatenate([gf, swap(gf, mask)])
        mask *= 2
    for stage in stages[1:] + stages[:1]:
        y = jnp.concatenate([y] + [swap(y, mask) for mask in stage])
    gf = gf.reshape(1, rows)
    own = (jnp.arange(cols_axis)[None, :, None] == col) & (row % (group // cols_axis) == 0)
    g = jnp.where(own, grad_g.reshape(rows_axis, 1, nt), 0.0).reshape(1, wide)

    br = min(256, rows, ELEMENTS // 4 // wide)
    vec = jax.ShapeDtypeStruct((1, wide), F32)
    line = jax.ShapeDtypeStruct((1, rows), F32)
    acc = pltpu.VMEM((8, wide), F32)
    block = pltpu.VMEM((br, wide), F32)
    depth = -(-(3 * features + 8) // 128) * 128
    plan = jax.ShapeDtypeStruct((rows, wide), BF16)
    lhs, rhs, yc, p, r, lse = call(
        functools.partial(lse_kernel, group, br),
        (me_ref, x, y),
        (
            jax.ShapeDtypeStruct((rows, depth), BF16),
            jax.ShapeDtypeStruct((depth, wide), BF16),
            jax.ShapeDtypeStruct((features + 16, wide), BF16),
            plan,
            jax.ShapeDtypeStruct((rows, 128), F32),
            vec,
        ),
        [block, block, acc, acc],
        smem=(0,),
        limit=32,
    )

    def join(values):
        top = functools.reduce(jnp.maximum, values)
        return top + jnp.log2(sum(jnp.exp2(v - top) for v in values))

    parts = exchange(lse, join)
    count = len(parts)
    p, scale, a, s = call(
        functools.partial(plan_kernel, count, math.log2(ns / nt)),
        (*parts, lhs, rhs, r, p),
        (plan, vec, line, vec),
        [],
        alias={count + 3: 0},
    )
    parts = exchange(s, sum)
    b, cm, m, u = call(
        functools.partial(rhs_kernel, count, ns / nt),
        (*parts, p, scale, gf, g),
        (vec, vec, line, vec),
        [],
    )
    state = ()
    for step in range(CG):
        parts = exchange(u, sum)
        *state, u = call(
            functools.partial(cg_kernel, count, step == 0),
            (*parts, p, scale, a, m, b, cm, *state),
            (vec, vec, vec, line, line, vec),
            [],
        )
    parts = exchange(u, sum)
    grad_src, part = call(
        functools.partial(grad_kernel, count, group),
        (*parts, me_ref, p, scale, a, m, b, cm, *state, gf, x, yc),
        (jax.ShapeDtypeStruct((features, ns), F32), jax.ShapeDtypeStruct((group, features, nt), F32)),
        [
            pltpu.VMEM((ns, wide), BF16),
            pltpu.VMEM((rows, group * nt), BF16),
            pltpu.VMEM((rows, 128), F32),
            pltpu.VMEM((rows, 128), F32),
        ],
        smem=(count,),
    )
    for stage in stages:
        size = len(stage) + 1
        unit = stage[0]
        part = part.reshape(part.shape[0] // size, size, features, nt)
        part = sum([swap(part[:, mask // unit], mask) for mask in stage], part[:, 0])
    return grad_src, part.reshape(features, nt)


def solution(mesh):
    in_specs = (P(None, ("row", "col")), P(None, ("col", "row")), P("row"), P("col"))
    out_specs = (P(None, ("row", "col")), P(None, ("col", "row")))
    return jax.shard_map(body, mesh=mesh, in_specs=in_specs, out_specs=out_specs, check_vma=False)
```

```python
import functools
import math

import jax
import jax.numpy as jnp
from jax import lax
from jax.experimental import pallas as pl
from jax.experimental.pallas import tpu as pltpu
from jax.sharding import PartitionSpec as P

CG = 3
EPS = 4.0
TAU = 0.1
AXES = ("row", "col")
LOW = -3.0e38
TINY = 2.0**-80
LIMIT = 80.0
SPAN = 4096
ELEMENTS = 4 * 1024 * 1024
LOG2E = math.log2(math.e)
CROSS = 2.0 * LOG2E / EPS
SQUARE = LOG2E / EPS
F32 = jnp.float32
BF16 = jnp.bfloat16
NT = (((1,), (1,)), ((), ()))
VMEM = pl.BlockSpec(memory_space=pltpu.VMEM)
SMEM = pl.BlockSpec(memory_space=pltpu.SMEM)


def split3(vector):
    high = vector.astype(BF16).astype(F32)
    rest = vector - high
    mid = rest.astype(BF16).astype(F32)
    low = rest - mid
    shape = (8, vector.shape[1])
    line = lax.broadcasted_iota(jnp.int32, shape, 0)
    zero = jnp.zeros(shape, F32)
    rows = jnp.where(line == 0, high, jnp.where(line == 1, mid, jnp.where(line == 2, low, zero)))
    return rows.astype(BF16)


def total(vector):
    return jnp.sum(vector, axis=1, keepdims=True)


def fold(rows):
    return jnp.sum(rows, axis=0, keepdims=True)


def down(vector):
    return jnp.broadcast_to(vector, (128, vector.shape[1])).T


def over(wide, step, carry):
    span = min(wide, SPAN)
    if wide == span:
        return step(0, carry)
    return lax.fori_loop(0, wide // span, lambda i, c: step(pl.multiple_of(i * span, span), c), carry)


def lanes(base, offset, size):
    return pl.ds(pl.multiple_of(base + offset, 128), size) if not isinstance(base, int) else pl.ds(base + offset, size)


def lse_kernel(
    group, br, me_ref, x_ref, y_ref, lhs_ref, rhs_ref, yc_ref, p_ref, r_ref, lse_ref, sa_ref, sb_ref, acc_ref, m_ref
):
    me = me_ref[0]
    replicas, _, ns = x_ref.shape
    devices, features, nt = y_ref.shape
    rows, wide = p_ref.shape
    extra = lhs_ref.shape[1] - 3 * features
    lhs_ref[:, 3 * features :] = jnp.ones((rows, extra), BF16)
    for k in range(replicas):
        points = x_ref[k, :features, :].T
        for c in range(3):
            lhs_ref[k * ns : (k + 1) * ns, c * features : (c + 1) * features] = points
    yc_ref[features:, :] = jnp.ones((yc_ref.shape[0] - features, wide), BF16)
    for t in range(devices):
        cs = slice(t * nt, (t + 1) * nt)
        k = jnp.bitwise_xor(t, me)
        inner = k % group
        points = y_ref[(inner % 2) * (devices // 2) + (inner // 2) * replicas + k // group]
        yc_ref[:features, cs] = points
        points = points.astype(F32)
        square = fold(points * points) * -SQUARE
        value = points * CROSS
        high = value.astype(BF16)
        rest = value - high.astype(F32)
        mid = rest.astype(BF16)
        rhs_ref[:features, cs] = high
        rhs_ref[features : 2 * features, cs] = mid
        rhs_ref[2 * features : 3 * features, cs] = (rest - mid.astype(F32)).astype(BF16)
        rhs_ref[3 * features : 3 * features + 8, cs] = split3(square)
        rhs_ref[3 * features + 8 :, cs] = jnp.zeros((extra - 8, nt), BF16)
    scratch = (sa_ref, sb_ref)

    def scores(b):
        lb = lhs_ref[b * br : (b + 1) * br, :]
        s_ref = scratch[b % 2]

        def step(base, high):
            for u in range(0, min(wide, SPAN), 256):
                cs = lanes(base, u, 256)
                s = jnp.dot(lb, rhs_ref[:, cs], preferred_element_type=F32)
                s_ref[:, cs] = s
                high = jnp.maximum(high, jnp.maximum(s[:, :128], s[:, 128:]))
            return high

        return jnp.max(over(wide, step, jnp.full((br, 128), LOW, F32)), axis=1, keepdims=True)

    def exps(b, high):
        s_ref = scratch[b % 2]
        rs = slice(b * br, (b + 1) * br)
        hb = jnp.broadcast_to(high, (br, 128))

        def step(base, acc):
            for u in range(0, min(wide, SPAN), 128):
                cs = lanes(base, u, 128)
                e = jnp.exp2(s_ref[:, cs] - hb)
                p_ref[rs, cs] = e.astype(BF16)
                acc = acc + e
            return acc

        sums = jnp.sum(over(wide, step, jnp.zeros((br, 128), F32)), axis=1, keepdims=True)
        r_ref[rs, :] = jnp.broadcast_to(-(high + jnp.log2(sums)), (br, 128))
        return jnp.broadcast_to(1.0 / sums, (br, 128)).T[:1]

    count = rows // br
    inverse = []
    high = scores(0)
    for b in range(count):
        after = scores(b + 1) if b + 1 < count else None
        inverse.append(exps(b, high))
        high = after
    s = pulled(p_ref, jnp.concatenate(inverse, axis=1))
    lse_ref[...] = jnp.log2(jnp.maximum(s, TINY))

    @pl.when(jnp.min(s) < TINY)
    def _():
        acc_ref[...] = jnp.zeros(acc_ref.shape, F32)
        m_ref[...] = jnp.full(m_ref.shape, LOW, F32)

        def step(i, _):
            rs, cs, v = tile_scores(i, lhs_ref, rhs_ref, r_ref)
            v = v.reshape(v.shape[0] // 8, 8, 128)
            old = m_ref[:, cs]
            new = jnp.maximum(old, jnp.max(v, axis=0))
            acc_ref[:, cs] = acc_ref[:, cs] * jnp.exp2(old - new) + fold3(jnp.exp2(v - new[None]))
            m_ref[:, cs] = new
            return 0

        lax.fori_loop(0, (rows // 128) * (wide // 128), step, 0)
        m = m_ref[...]
        top = jnp.max(m, axis=0, keepdims=True)
        lse_ref[...] = top + jnp.log2(fold(acc_ref[...] * jnp.exp2(m - top)))


def fold3(values):
    return jnp.sum(values, axis=0)


def tile_scores(i, lhs_ref, rhs_ref, r_ref):
    across = rhs_ref.shape[1] // 128
    rs = pl.ds(pl.multiple_of(i // across * 128, 128), 128)
    cs = pl.ds(pl.multiple_of(i % across * 128, 128), 128)
    return rs, cs, jnp.dot(lhs_ref[rs, :], rhs_ref[:, cs], preferred_element_type=F32) + r_ref[rs, :]


def pushed(p_ref, w):
    return fold(lax.dot_general(split3(w), p_ref[...], NT, preferred_element_type=F32))


def pulled(p_ref, y):
    return fold(jnp.dot(split3(y), p_ref[...], preferred_element_type=F32))


def plan_kernel(count, shift, *refs):
    parts, (lhs_ref, rhs_ref, r_ref, old_ref, p_ref, scale_ref, a_ref, s_ref) = refs[:count], refs[count:]
    top = functools.reduce(jnp.maximum, [q[...] for q in parts])
    c = shift - top - jnp.log2(sum(jnp.exp2(q[...] - top) for q in parts))
    rows, wide = p_ref.shape
    plain = jnp.max(c) <= LIMIT
    scale_ref[...] = jnp.exp2(jnp.minimum(c, LIMIT))

    @pl.when(jnp.logical_not(plain))
    def _():
        scale_ref[...] = c

        def step(i, _):
            rs, cs, v = tile_scores(i, lhs_ref, rhs_ref, r_ref)
            p_ref[rs, cs] = jnp.exp2(v + scale_ref[:, cs]).astype(BF16)
            return 0

        lax.fori_loop(0, (rows // 128) * (wide // 128), step, 0)
        scale_ref[...] = jnp.ones((1, wide), F32)

    scale = scale_ref[...]
    a = 1.0 / pushed(p_ref, scale)
    a_ref[...] = a
    s_ref[...] = scale * pulled(p_ref, a)


def rhs_kernel(count, ratio, *refs):
    parts, (p_ref, scale_ref, gf_ref, g_ref, b_ref, cm_ref, m_ref, out_ref) = refs[:count], refs[count:]
    s = sum(q[...] for q in parts)
    b = ratio / s
    b_ref[...] = b
    cm_ref[...] = b * s

    scale = scale_ref[...]
    m = pushed(p_ref, scale * b)
    m_ref[...] = m
    out_ref[...] = g_ref[...] - b * scale * pulled(p_ref, gf_ref[...] / m)


def advance(parts, b, cm, dual, residual, direction):
    image = (1.0 + TAU) * cm * direction - b * sum(q[...] for q in parts)
    alpha = total(residual * residual) / total(direction * image)
    return alpha, dual + alpha * direction, residual - alpha * image


def cg_kernel(count, first, *refs):
    parts, refs = refs[:count], refs[count:]
    p_ref, scale_ref, a_ref, m_ref, b_ref, cm_ref = refs[:6]
    b = b_ref[...]
    if first:
        out = refs[6:]
        direction = sum(q[...] for q in parts)
        residual = direction
        dual = jnp.zeros_like(direction)
        mix = jnp.zeros(a_ref.shape, F32)
    else:
        dual_ref, res_ref, dir_ref, q_ref, mix_ref = refs[6:11]
        out = refs[11:]
        old = res_ref[...]
        before = dir_ref[...]
        alpha, dual, residual = advance(parts, b, cm_ref[...], dual_ref[...], old, before)
        direction = residual + total(residual * residual) / total(old * old) * before
        mix = mix_ref[...] + alpha * q_ref[...]
    dual_out, res_out, dir_out, q_out, mix_out, u_out = out
    dual_out[...] = dual
    res_out[...] = residual
    dir_out[...] = direction
    mix_out[...] = mix

    scale = scale_ref[...]
    q = pushed(p_ref, scale * b * direction)
    q_out[...] = q
    u_out[...] = scale * pulled(p_ref, a_ref[...] * q / m_ref[...])


def grad_kernel(count, group, *refs):
    parts, refs = refs[:count], refs[count:]
    me_ref, p_ref, scale_ref, a_ref, m_ref, b_ref, cm_ref, dual_ref, res_ref, dir_ref, q_ref, mix_ref = refs[:12]
    gf_ref, x_ref, yc_ref, srca_ref, srcb_ref, tgt_ref, step_ref = refs[12:19]
    wa_ref, wb_ref, va_ref, vb_ref, ad_ref, da_ref, db_ref = refs[19:]
    me = me_ref[0]
    replicas, _, ns = x_ref.shape
    features = srca_ref.shape[0]
    nt = tgt_ref.shape[2]
    b = b_ref[...]
    cm = cm_ref[...]
    old = res_ref[...]
    before = dir_ref[...]
    alpha, dual, residual = advance(parts, b, cm, dual_ref[...], old, before)
    norm = total(residual * residual)
    direction = residual + norm / total(old * old) * before
    a = a_ref[...]
    m = m_ref[...]
    mix = mix_ref[...] + alpha * q_ref[...]
    b = b * scale_ref[...]
    q = pushed(p_ref, b * direction)
    ad_ref[...] = down(a)
    da_ref[...] = down((gf_ref[...] / a - mix) / m)
    db_ref[...] = down(-q / m)
    step_ref[0:1, :] = jnp.broadcast_to(norm, (1, 128))
    step_ref[1:2, :] = jnp.broadcast_to(total((1.0 + TAU) * cm * direction * direction), (1, 128))
    taken = total(a * q * q / m)
    wide = b.shape[1]
    half = group * nt
    base = (me // group) * half

    def weigh(rows, source, bs, duals, dirs, outs):
        plan = source.astype(F32) * (ad_ref[rows, :] * bs)
        outs[0][...] = (plan * (da_ref[rows, :] + duals)).astype(BF16)
        outs[1][...] = (plan * (db_ref[rows, :] + dirs)).astype(BF16)

    for u in range(wide // 128):
        cs = slice(u * 128, (u + 1) * 128)
        weigh(slice(0, ns), p_ref[:ns, cs], b[:, cs], dual[:, cs], direction[:, cs], (wa_ref.at[:, cs], wb_ref.at[:, cs]))
    own = x_ref[0, :features, :].astype(F32)
    for w_ref, out_ref in ((wa_ref, srca_ref), (wb_ref, srcb_ref)):
        out = lax.dot_general(yc_ref[...], w_ref[...], NT, preferred_element_type=F32)
        out_ref[...] = 2.0 * (own * out[features : features + 1] - out[:features])

    b, dual, direction = [pick(v, me // group, half) for v in (b, dual, direction)]
    for u in range(half // 128):
        cs = slice(u * 128, (u + 1) * 128)
        cd = pl.ds(pl.multiple_of(base + u * 128, 128), 128)
        weigh(slice(None), p_ref[:, cd], b[:, cs], dual[:, cs], direction[:, cs], (va_ref.at[:, cs], vb_ref.at[:, cs]))
    mine = yc_ref[:features, pl.ds(pl.multiple_of(base, 128), half)].astype(F32)
    ones = jnp.ones((8, va_ref.shape[0]), BF16)
    for c, w_ref in enumerate((va_ref, vb_ref)):
        sums = jnp.zeros((features, half), F32)
        for k in range(replicas):
            rows = slice(k * ns, (k + 1) * ns)
            sums = sums + jnp.dot(x_ref[k, :features, :], w_ref[rows, :], preferred_element_type=F32)
        part = 2.0 * (mine * jnp.dot(ones, w_ref[...], preferred_element_type=F32)[:1] - sums)
        for k in range(group):
            slot = jnp.bitwise_xor(k, me % group)
            tgt_ref[slot, c * features : (c + 1) * features, :] = part[:, k * nt : (k + 1) * nt]
    for k in range(group):
        tgt_ref[k, 2 * features :, :] = jnp.broadcast_to(taken, (8, nt))


def last_kernel(count, *refs):
    parts, (srca_ref, srcb_ref, step_ref, src_ref, tgt_ref) = refs[:count], refs[count:]
    features = src_ref.shape[0]
    rows = sum(q[0] for q in parts)
    alpha = step_ref[0:1, 0:1] / (step_ref[1:2, 0:1] - rows[2 * features : 2 * features + 1, 0:1])
    src_ref[...] = srca_ref[...] + alpha * srcb_ref[...]
    tgt_ref[...] = rows[:features] + alpha * rows[features : 2 * features]


def pick(vector, index, size):
    out = vector[:, :size]
    for k in range(1, vector.shape[1] // size):
        out = jnp.where(index == k, vector[:, k * size : (k + 1) * size], out)
    return out


def call(kernel, operands, outs, scratch, smem=(), limit=24, alias={}):
    return pl.pallas_call(
        kernel,
        out_shape=outs,
        in_specs=[SMEM if i in smem else VMEM for i in range(len(operands))],
        out_specs=[VMEM] * len(outs),
        scratch_shapes=scratch,
        input_output_aliases=alias,
        compiler_params=pltpu.CompilerParams(vmem_limit_bytes=limit * 1024 * 1024),
    )(*operands)


def body(src_points, tgt_points, grad_f, grad_g):
    rows_axis, cols_axis = lax.axis_size("row"), lax.axis_size("col")
    devices = rows_axis * cols_axis
    features, ns = src_points.shape
    nt = tgt_points.shape[1]
    wide = devices * nt
    group = 2
    while group < devices and devices // group * ns * wide > ELEMENTS:
        group *= 2
    replicas = devices // group
    rows = replicas * ns
    row, col = lax.axis_index("row"), lax.axis_index("col")
    me = row * cols_axis + col
    me_ref = me.astype(jnp.int32).reshape(1)

    def swap(value, mask):
        return lax.ppermute(value, AXES, [(i, i ^ mask) for i in range(devices)])

    bits = [1 << i for i in range(1, group.bit_length() - 1)]
    stages = [[1]]
    for i in range(0, len(bits), 2):
        pair = bits[i : i + 2]
        stages.append(([pair[0] | pair[1]] if len(pair) == 2 else []) + pair[::-1])

    def exchange(value, combine):
        for stage in stages[:-1]:
            value = combine([value] + [swap(value, mask) for mask in stage])
        return [value] + [swap(value, mask) for mask in stages[-1]]

    y = tgt_points[None]
    gf = lax.dynamic_slice(grad_f, (col * ns,), (ns,))[None]
    x = src_points[None]
    mask = group
    while mask < devices:
        y = jnp.concatenate([y, swap(y, mask)])
        x = jnp.concatenate([x, swap(x, mask)])
        gf = jnp.concatenate([gf, swap(gf, mask)])
        mask *= 2
    for stage in stages[1:] + stages[:1]:
        sent = {0: y} | {mask // stage[-1]: swap(y, mask) for mask in stage}
        y = jnp.concatenate([sent[k] for k in range(len(sent))])
    gf = gf.reshape(1, rows)
    own = (jnp.arange(cols_axis)[None, :, None] == col) & (row % (group // cols_axis) == 0)
    g = jnp.where(own, grad_g.reshape(rows_axis, 1, nt), 0.0).reshape(1, wide)

    br = min(256, rows, ELEMENTS // 4 // wide)
    vec = jax.ShapeDtypeStruct((1, wide), F32)
    line = jax.ShapeDtypeStruct((1, rows), F32)
    acc = pltpu.VMEM((8, wide), F32)
    block = pltpu.VMEM((br, wide), F32)
    depth = -(-(3 * features + 8) // 128) * 128
    plan = jax.ShapeDtypeStruct((rows, wide), BF16)
    lhs, rhs, yc, p, r, lse = call(
        functools.partial(lse_kernel, group, br),
        (me_ref, x, y),
        (
            jax.ShapeDtypeStruct((rows, depth), BF16),
            jax.ShapeDtypeStruct((depth, wide), BF16),
            jax.ShapeDtypeStruct((features + 16, wide), BF16),
            plan,
            jax.ShapeDtypeStruct((rows, 128), F32),
            vec,
        ),
        [block, block, acc, acc],
        smem=(0,),
        limit=32,
    )

    def join(values):
        top = functools.reduce(jnp.maximum, values)
        return top + jnp.log2(sum(jnp.exp2(v - top) for v in values))

    parts = exchange(lse, join)
    count = len(parts)
    p, scale, a, s = call(
        functools.partial(plan_kernel, count, math.log2(ns / nt)),
        (*parts, lhs, rhs, r, p),
        (plan, vec, line, vec),
        [],
        alias={count + 3: 0},
    )
    parts = exchange(s, sum)
    b, cm, m, u = call(
        functools.partial(rhs_kernel, count, ns / nt),
        (*parts, p, scale, gf, g),
        (vec, vec, line, vec),
        [],
    )
    state = ()
    for step in range(CG - 1):
        parts = exchange(u, sum)
        *state, u = call(
            functools.partial(cg_kernel, count, step == 0),
            (*parts, p, scale, a, m, b, cm, *state),
            (vec, vec, vec, line, line, vec),
            [],
        )
    parts = exchange(u, sum)
    grad = jax.ShapeDtypeStruct((features, ns), F32)
    srca, srcb, part, scalars = call(
        functools.partial(grad_kernel, count, group),
        (*parts, me_ref, p, scale, a, m, b, cm, *state, gf, x, yc),
        (
            grad,
            grad,
            jax.ShapeDtypeStruct((group, 2 * features + 8, nt), F32),
            jax.ShapeDtypeStruct((8, 128), F32),
        ),
        [pltpu.VMEM((ns, wide), BF16)] * 2
        + [pltpu.VMEM((rows, group * nt), BF16)] * 2
        + [pltpu.VMEM((rows, 128), F32)] * 3,
        smem=(count,),
    )
    for stage in stages:
        size = len(stage) + 1
        part = part.reshape(part.shape[0] // size, size, *part.shape[1:])
        pieces = [part[:, 0]] + [swap(part[:, mask // stage[-1]], mask) for mask in stage]
        part = sum(pieces[1:], pieces[0]) if stage is not stages[-1] else part
    return call(
        functools.partial(last_kernel, len(pieces)),
        (*pieces, srca, srcb, scalars),
        (grad, jax.ShapeDtypeStruct((features, nt), F32)),
        [],
    )


def solution(mesh):
    in_specs = (P(None, ("row", "col")), P(None, ("col", "row")), P("row"), P("col"))
    out_specs = (P(None, ("row", "col")), P(None, ("col", "row")))
    return jax.shard_map(body, mesh=mesh, in_specs=in_specs, out_specs=out_specs, check_vma=False)
```

```python
import functools
import math

import jax
import jax.numpy as jnp
from jax import lax
from jax.experimental import pallas as pl
from jax.experimental.pallas import tpu as pltpu
from jax.sharding import PartitionSpec as P


CG = 3
EPS = 4.0
TAU = 0.1
AXES = ("row", "col")
LOW = -3.0e38
TINY = 2.0**-80
LIMIT = 80.0
SPAN = 4096
ELEMENTS = 4 * 1024 * 1024
LOG2E = math.log2(math.e)
CROSS = 2.0 * LOG2E / EPS
SQUARE = LOG2E / EPS
F32 = jnp.float32
BF16 = jnp.bfloat16
NT = (((1,), (1,)), ((), ()))
VMEM = pl.BlockSpec(memory_space=pltpu.VMEM)
SMEM = pl.BlockSpec(memory_space=pltpu.SMEM)


def split3(vector):
    high = vector.astype(BF16).astype(F32)
    rest = vector - high
    mid = rest.astype(BF16).astype(F32)
    low = rest - mid
    shape = (8, vector.shape[1])
    line = lax.broadcasted_iota(jnp.int32, shape, 0)
    zero = jnp.zeros(shape, F32)
    rows = jnp.where(line == 0, high, jnp.where(line == 1, mid, jnp.where(line == 2, low, zero)))
    return rows.astype(BF16)


def total(vector):
    return jnp.sum(vector, axis=1, keepdims=True)


def fold(rows):
    return jnp.sum(rows, axis=0, keepdims=True)


def down(vector):
    return jnp.broadcast_to(vector, (128, vector.shape[1])).T


def over(wide, step, carry):
    span = min(wide, SPAN)
    if wide == span:
        return step(0, carry)
    return lax.fori_loop(0, wide // span, lambda i, c: step(pl.multiple_of(i * span, span), c), carry)


def lanes(base, offset, size):
    return pl.ds(pl.multiple_of(base + offset, 128), size) if not isinstance(base, int) else pl.ds(base + offset, size)


def pack_kernel(columns, me_ref, src_ref, tgt_ref, gf_ref, x_ref, y_ref, f_ref):
    f_ref[...] = pick(gf_ref[...], me_ref[0] % columns, src_ref.shape[1])
    x_ref[0] = src_ref[...]
    y_ref[0] = tgt_ref[...]


def lse_kernel(
    group, br, me_ref, x_ref, y_ref, lhs_ref, rhs_ref, yc_ref, p_ref, r_ref, lse_ref, sa_ref, sb_ref, acc_ref, m_ref
):
    me = me_ref[0]
    replicas, _, ns = x_ref.shape
    devices, features, nt = y_ref.shape
    rows, wide = p_ref.shape
    extra = lhs_ref.shape[1] - 3 * features
    lhs_ref[:, 3 * features :] = jnp.ones((rows, extra), BF16)
    for k in range(replicas):
        points = x_ref[k, :features, :].T
        for c in range(3):
            lhs_ref[k * ns : (k + 1) * ns, c * features : (c + 1) * features] = points
    yc_ref[features:, :] = jnp.ones((yc_ref.shape[0] - features, wide), BF16)
    for t in range(devices):
        cs = slice(t * nt, (t + 1) * nt)
        k = jnp.bitwise_xor(t, me)
        inner = k % group
        points = y_ref[(inner % 2) * (devices // 2) + (inner // 2) * replicas + k // group]
        yc_ref[:features, cs] = points
        points = points.astype(F32)
        square = fold(points * points) * -SQUARE
        value = points * CROSS
        high = value.astype(BF16)
        rest = value - high.astype(F32)
        mid = rest.astype(BF16)
        rhs_ref[:features, cs] = high
        rhs_ref[features : 2 * features, cs] = mid
        rhs_ref[2 * features : 3 * features, cs] = (rest - mid.astype(F32)).astype(BF16)
        rhs_ref[3 * features : 3 * features + 8, cs] = split3(square)
        rhs_ref[3 * features + 8 :, cs] = jnp.zeros((extra - 8, nt), BF16)
    scratch = (sa_ref, sb_ref)

    def scores(b):
        lb = lhs_ref[b * br : (b + 1) * br, :]
        s_ref = scratch[b % 2]

        def step(base, high):
            for u in range(0, min(wide, SPAN), 256):
                cs = lanes(base, u, 256)
                s = jnp.dot(lb, rhs_ref[:, cs], preferred_element_type=F32)
                s_ref[:, cs] = s
                high = jnp.maximum(high, jnp.maximum(s[:, :128], s[:, 128:]))
            return high

        return jnp.max(over(wide, step, jnp.full((br, 128), LOW, F32)), axis=1, keepdims=True)

    def exps(b, high):
        s_ref = scratch[b % 2]
        rs = slice(b * br, (b + 1) * br)
        hb = jnp.broadcast_to(high, (br, 128))

        def step(base, acc):
            for u in range(0, min(wide, SPAN), 128):
                cs = lanes(base, u, 128)
                e = jnp.exp2(s_ref[:, cs] - hb)
                p_ref[rs, cs] = e.astype(BF16)
                acc = acc + e
            return acc

        sums = jnp.sum(over(wide, step, jnp.zeros((br, 128), F32)), axis=1, keepdims=True)
        r_ref[rs, :] = jnp.broadcast_to(-(high + jnp.log2(sums)), (br, 128))
        return jnp.broadcast_to(1.0 / sums, (br, 128)).T[:1]

    count = rows // br
    inverse = []
    high = scores(0)
    for b in range(count):
        after = scores(b + 1) if b + 1 < count else None
        inverse.append(exps(b, high))
        high = after
    s = pulled(p_ref, jnp.concatenate(inverse, axis=1))
    lse_ref[...] = jnp.log2(jnp.maximum(s, TINY))

    @pl.when(jnp.min(s) < TINY)
    def _():
        acc_ref[...] = jnp.zeros(acc_ref.shape, F32)
        m_ref[...] = jnp.full(m_ref.shape, LOW, F32)

        def step(i, _):
            _, cs, v = tile_scores(i, lhs_ref, rhs_ref, r_ref)
            v = v.reshape(v.shape[0] // 8, 8, 128)
            old = m_ref[:, cs]
            new = jnp.maximum(old, jnp.max(v, axis=0))
            acc_ref[:, cs] = acc_ref[:, cs] * jnp.exp2(old - new) + fold3(jnp.exp2(v - new[None]))
            m_ref[:, cs] = new
            return 0

        lax.fori_loop(0, (rows // 128) * (wide // 128), step, 0)
        m = m_ref[...]
        top = jnp.max(m, axis=0, keepdims=True)
        lse_ref[...] = top + jnp.log2(fold(acc_ref[...] * jnp.exp2(m - top)))


def fold3(values):
    return jnp.sum(values, axis=0)


def tile_scores(i, lhs_ref, rhs_ref, r_ref):
    across = rhs_ref.shape[1] // 128
    rs = pl.ds(pl.multiple_of(i // across * 128, 128), 128)
    cs = pl.ds(pl.multiple_of(i % across * 128, 128), 128)
    return rs, cs, jnp.dot(lhs_ref[rs, :], rhs_ref[:, cs], preferred_element_type=F32) + r_ref[rs, :]


def pushed(p_ref, w):
    return fold(lax.dot_general(split3(w), p_ref[...], NT, preferred_element_type=F32))


def pulled(p_ref, y):
    return fold(jnp.dot(split3(y), p_ref[...], preferred_element_type=F32))


def plan_kernel(count, shift, *refs):
    parts, (lhs_ref, rhs_ref, r_ref, old_ref, p_ref, scale_ref, a_ref, s_ref) = refs[:count], refs[count:]
    top = functools.reduce(jnp.maximum, [q[...] for q in parts])
    c = shift - top - jnp.log2(sum(jnp.exp2(q[...] - top) for q in parts))
    rows, wide = p_ref.shape
    plain = jnp.max(c) <= LIMIT
    scale_ref[...] = jnp.exp2(jnp.minimum(c, LIMIT))

    @pl.when(jnp.logical_not(plain))
    def _():
        scale_ref[...] = c

        def step(i, _):
            rs, cs, v = tile_scores(i, lhs_ref, rhs_ref, r_ref)
            p_ref[rs, cs] = jnp.exp2(v + scale_ref[:, cs]).astype(BF16)
            return 0

        lax.fori_loop(0, (rows // 128) * (wide // 128), step, 0)
        scale_ref[...] = jnp.ones((1, wide), F32)

    scale = scale_ref[...]
    a = 1.0 / pushed(p_ref, scale)
    a_ref[...] = a
    s_ref[...] = scale * pulled(p_ref, a)


def rhs_kernel(count, ratio, *refs):
    parts, (p_ref, scale_ref, gf_ref, g_ref, b_ref, cm_ref, m_ref, out_ref) = refs[:count], refs[count:]
    s = sum(q[...] for q in parts)
    b = ratio / s
    b_ref[...] = b
    cm_ref[...] = b * s

    scale = scale_ref[...]
    m = pushed(p_ref, scale * b)
    m_ref[...] = m
    out_ref[...] = g_ref[...] - b * scale * pulled(p_ref, gf_ref[...] / m)


def advance(parts, b, cm, dual, residual, direction):
    image = (1.0 + TAU) * cm * direction - b * sum(q[...] for q in parts)
    alpha = total(residual * residual) / total(direction * image)
    return alpha, dual + alpha * direction, residual - alpha * image


def cg_kernel(count, first, *refs):
    parts, refs = refs[:count], refs[count:]
    p_ref, scale_ref, a_ref, m_ref, b_ref, cm_ref = refs[:6]
    b = b_ref[...]
    if first:
        out = refs[6:]
        direction = sum(q[...] for q in parts)
        residual = direction
        dual = jnp.zeros_like(direction)
        mix = jnp.zeros(a_ref.shape, F32)
    else:
        dual_ref, res_ref, dir_ref, q_ref, mix_ref = refs[6:11]
        out = refs[11:]
        old = res_ref[...]
        before = dir_ref[...]
        alpha, dual, residual = advance(parts, b, cm_ref[...], dual_ref[...], old, before)
        direction = residual + total(residual * residual) / total(old * old) * before
        mix = mix_ref[...] + alpha * q_ref[...]
    dual_out, res_out, dir_out, q_out, mix_out, u_out = out
    dual_out[...] = dual
    res_out[...] = residual
    dir_out[...] = direction
    mix_out[...] = mix

    scale = scale_ref[...]
    q = pushed(p_ref, scale * b * direction)
    q_out[...] = q
    u_out[...] = scale * pulled(p_ref, a_ref[...] * q / m_ref[...])


def grad_kernel(count, group, *refs):
    parts, refs = refs[:count], refs[count:]
    me_ref, p_ref, scale_ref, a_ref, m_ref, b_ref, cm_ref, dual_ref, res_ref, dir_ref, q_ref, mix_ref = refs[:12]
    gf_ref, x_ref, yc_ref, srca_ref, srcb_ref, tgt_ref, step_ref = refs[12:19]
    wa_ref, wb_ref, va_ref, vb_ref, ad_ref, da_ref, db_ref = refs[19:]
    me = me_ref[0]
    replicas, _, ns = x_ref.shape
    features = srca_ref.shape[0]
    nt = tgt_ref.shape[2]
    b = b_ref[...]
    cm = cm_ref[...]
    old = res_ref[...]
    before = dir_ref[...]
    alpha, dual, residual = advance(parts, b, cm, dual_ref[...], old, before)
    norm = total(residual * residual)
    direction = residual + norm / total(old * old) * before
    a = a_ref[...]
    m = m_ref[...]
    mix = mix_ref[...] + alpha * q_ref[...]
    b = b * scale_ref[...]
    q = pushed(p_ref, b * direction)
    ad_ref[...] = down(a)
    da_ref[...] = down((gf_ref[...] / a - mix) / m)
    db_ref[...] = down(-q / m)
    step_ref[0:1, :] = jnp.broadcast_to(norm, (1, 128))
    step_ref[1:2, :] = jnp.broadcast_to(total((1.0 + TAU) * cm * direction * direction), (1, 128))
    taken = total(a * q * q / m)
    wide = b.shape[1]
    half = group * nt
    base = (me // group) * half

    def weigh(rows, source, bs, duals, dirs, outs):
        plan = source.astype(F32) * (ad_ref[rows, :] * bs)
        outs[0][...] = (plan * (da_ref[rows, :] + duals)).astype(BF16)
        outs[1][...] = (plan * (db_ref[rows, :] + dirs)).astype(BF16)

    for u in range(wide // 128):
        cs = slice(u * 128, (u + 1) * 128)
        weigh(slice(0, ns), p_ref[:ns, cs], b[:, cs], dual[:, cs], direction[:, cs], (wa_ref.at[:, cs], wb_ref.at[:, cs]))
    own = x_ref[0, :features, :].astype(F32)
    for w_ref, out_ref in ((wa_ref, srca_ref), (wb_ref, srcb_ref)):
        out = lax.dot_general(yc_ref[...], w_ref[...], NT, preferred_element_type=F32)
        out_ref[...] = 2.0 * (own * out[features : features + 1] - out[:features])

    b, dual, direction = [pick(v, me // group, half) for v in (b, dual, direction)]
    for u in range(half // 128):
        cs = slice(u * 128, (u + 1) * 128)
        cd = pl.ds(pl.multiple_of(base + u * 128, 128), 128)
        weigh(slice(None), p_ref[:, cd], b[:, cs], dual[:, cs], direction[:, cs], (va_ref.at[:, cs], vb_ref.at[:, cs]))
    mine = yc_ref[:features, pl.ds(pl.multiple_of(base, 128), half)].astype(F32)
    ones = jnp.ones((8, va_ref.shape[0]), BF16)
    for c, w_ref in enumerate((va_ref, vb_ref)):
        sums = jnp.zeros((features, half), F32)
        for k in range(replicas):
            rows = slice(k * ns, (k + 1) * ns)
            sums = sums + jnp.dot(x_ref[k, :features, :], w_ref[rows, :], preferred_element_type=F32)
        part = 2.0 * (mine * jnp.dot(ones, w_ref[...], preferred_element_type=F32)[:1] - sums)
        for k in range(group):
            slot = jnp.bitwise_xor(k, me % group)
            tgt_ref[slot, c * features : (c + 1) * features, :] = part[:, k * nt : (k + 1) * nt]
    for k in range(group):
        tgt_ref[k, 2 * features :, :] = jnp.broadcast_to(taken, (8, nt))


def last_kernel(count, *refs):
    parts, (srca_ref, srcb_ref, step_ref, src_ref, tgt_ref) = refs[:count], refs[count:]
    features = src_ref.shape[0]
    rows = sum(q[0] for q in parts)
    alpha = step_ref[0:1, 0:1] / (step_ref[1:2, 0:1] - rows[2 * features : 2 * features + 1, 0:1])
    src_ref[...] = srca_ref[...] + alpha * srcb_ref[...]
    tgt_ref[...] = rows[:features] + alpha * rows[features : 2 * features]


def pick(vector, index, size):
    out = vector[:, :size]
    for k in range(1, vector.shape[1] // size):
        out = jnp.where(index == k, vector[:, k * size : (k + 1) * size], out)
    return out


def call(kernel, operands, outs, scratch, smem=(), limit=24, alias={}):
    return pl.pallas_call(
        kernel,
        out_shape=outs,
        in_specs=[SMEM if i in smem else VMEM for i in range(len(operands))],
        out_specs=[VMEM] * len(outs),
        scratch_shapes=scratch,
        input_output_aliases=alias,
        compiler_params=pltpu.CompilerParams(vmem_limit_bytes=limit * 1024 * 1024),
    )(*operands)


def body(src_points, tgt_points, grad_f, grad_g):
    rows_axis, cols_axis = lax.axis_size("row"), lax.axis_size("col")
    devices = rows_axis * cols_axis
    features, ns = src_points.shape
    nt = tgt_points.shape[1]
    wide = devices * nt
    group = 2
    while group < devices and devices // group * ns * wide > ELEMENTS:
        group *= 2
    replicas = devices // group
    rows = replicas * ns
    row, col = lax.axis_index("row"), lax.axis_index("col")
    me = row * cols_axis + col
    me_ref = me.astype(jnp.int32).reshape(1)

    def swap(value, mask):
        return lax.ppermute(value, AXES, [(i, i ^ mask) for i in range(devices)])

    bits = [1 << i for i in range(1, group.bit_length() - 1)]
    stages = [[1]]
    for i in range(0, len(bits), 2):
        pair = bits[i : i + 2]
        stages.append(([pair[0] | pair[1]] if len(pair) == 2 else []) + pair[::-1])

    def exchange(value, combine):
        for stage in stages[:-1]:
            value = combine([value] + [swap(value, mask) for mask in stage])
        return [value] + [swap(value, mask) for mask in stages[-1]]

    x, y, gf = call(
        functools.partial(pack_kernel, cols_axis),
        (me_ref, src_points, tgt_points, grad_f.reshape(1, -1)),
        (
            jax.ShapeDtypeStruct((1, features, ns), BF16),
            jax.ShapeDtypeStruct((1, features, nt), BF16),
            jax.ShapeDtypeStruct((1, ns), F32),
        ),
        [],
        smem=(0,),
        limit=4,
    )
    mask = group
    while mask < devices:
        y = jnp.concatenate([y, swap(y, mask)])
        x = jnp.concatenate([x, swap(x, mask)])
        gf = jnp.concatenate([gf, swap(gf, mask)])
        mask *= 2
    for stage in stages[1:] + stages[:1]:
        sent = {0: y} | {mask // stage[-1]: swap(y, mask) for mask in stage}
        y = jnp.concatenate([sent[k] for k in range(len(sent))])
    gf = gf.reshape(1, rows)
    own = (jnp.arange(cols_axis)[None, :, None] == col) & (row % (group // cols_axis) == 0)
    g = jnp.where(own, grad_g.reshape(rows_axis, 1, nt), 0.0).reshape(1, wide)

    br = min(256, rows, ELEMENTS // 4 // wide)
    vec = jax.ShapeDtypeStruct((1, wide), F32)
    line = jax.ShapeDtypeStruct((1, rows), F32)
    acc = pltpu.VMEM((8, wide), F32)
    block = pltpu.VMEM((br, wide), F32)
    depth = -(-(3 * features + 8) // 128) * 128
    plan = jax.ShapeDtypeStruct((rows, wide), BF16)
    lhs, rhs, yc, p, r, lse = call(
        functools.partial(lse_kernel, group, br),
        (me_ref, x, y),
        (
            jax.ShapeDtypeStruct((rows, depth), BF16),
            jax.ShapeDtypeStruct((depth, wide), BF16),
            jax.ShapeDtypeStruct((features + 16, wide), BF16),
            plan,
            jax.ShapeDtypeStruct((rows, 128), F32),
            vec,
        ),
        [block, block, acc, acc],
        smem=(0,),
        limit=32,
    )

    def join(values):
        top = functools.reduce(jnp.maximum, values)
        return top + jnp.log2(sum(jnp.exp2(v - top) for v in values))

    parts = exchange(lse, join)
    count = len(parts)
    p, scale, a, s = call(
        functools.partial(plan_kernel, count, math.log2(ns / nt)),
        (*parts, lhs, rhs, r, p),
        (plan, vec, line, vec),
        [],
        alias={count + 3: 0},
    )
    parts = exchange(s, sum)
    b, cm, m, u = call(
        functools.partial(rhs_kernel, count, ns / nt),
        (*parts, p, scale, gf, g),
        (vec, vec, line, vec),
        [],
    )
    state = ()
    for step in range(CG - 1):
        parts = exchange(u, sum)
        *state, u = call(
            functools.partial(cg_kernel, count, step == 0),
            (*parts, p, scale, a, m, b, cm, *state),
            (vec, vec, vec, line, line, vec),
            [],
        )
    parts = exchange(u, sum)
    grad = jax.ShapeDtypeStruct((features, ns), F32)
    srca, srcb, part, scalars = call(
        functools.partial(grad_kernel, count, group),
        (*parts, me_ref, p, scale, a, m, b, cm, *state, gf, x, yc),
        (
            grad,
            grad,
            jax.ShapeDtypeStruct((group, 2 * features + 8, nt), F32),
            jax.ShapeDtypeStruct((8, 128), F32),
        ),
        [pltpu.VMEM((ns, wide), BF16)] * 2
        + [pltpu.VMEM((rows, group * nt), BF16)] * 2
        + [pltpu.VMEM((rows, 128), F32)] * 3,
        smem=(count,),
    )
    for stage in stages:
        size = len(stage) + 1
        part = part.reshape(part.shape[0] // size, size, *part.shape[1:])
        pieces = [part[:, 0]] + [swap(part[:, mask // stage[-1]], mask) for mask in stage]
        part = sum(pieces[1:], pieces[0]) if stage is not stages[-1] else part
    return call(
        functools.partial(last_kernel, len(pieces)),
        (*pieces, srca, srcb, scalars),
        (grad, jax.ShapeDtypeStruct((features, nt), F32)),
        [],
    )


def solution(mesh):
    in_specs = (P(None, ("row", "col")), P(None, ("col", "row")), P("row"), P("col"))
    out_specs = (P(None, ("row", "col")), P(None, ("col", "row")))

    return jax.shard_map(body, mesh=mesh, in_specs=in_specs, out_specs=out_specs, check_vma=False)
```

```python
import functools
import math

import jax
import jax.numpy as jnp
from jax import lax
from jax.experimental import pallas as pl
from jax.experimental.pallas import tpu as pltpu
from jax.sharding import PartitionSpec as P


CG = 3
EPS = 4.0
TAU = 0.1
AXES = ("row", "col")
LOW = -3.0e38
TINY = 2.0**-80
LIMIT = 80.0
SPAN = 4096
ELEMENTS = 4 * 1024 * 1024
LOG2E = math.log2(math.e)
CROSS = 2.0 * LOG2E / EPS
SQUARE = LOG2E / EPS
F32 = jnp.float32
BF16 = jnp.bfloat16
NT = (((1,), (1,)), ((), ()))
VMEM = pl.BlockSpec(memory_space=pltpu.VMEM)
SMEM = pl.BlockSpec(memory_space=pltpu.SMEM)


def split3(vector):
    high = vector.astype(BF16).astype(F32)
    rest = vector - high
    mid = rest.astype(BF16).astype(F32)
    low = rest - mid
    shape = (8, vector.shape[1])
    line = lax.broadcasted_iota(jnp.int32, shape, 0)
    zero = jnp.zeros(shape, F32)
    rows = jnp.where(line == 0, high, jnp.where(line == 1, mid, jnp.where(line == 2, low, zero)))
    return rows.astype(BF16)


def total(vector):
    return jnp.sum(vector, axis=1, keepdims=True)


def fold(rows):
    return jnp.sum(rows, axis=0, keepdims=True)


def down(vector):
    return jnp.broadcast_to(vector, (128, vector.shape[1])).T


def over(wide, step, carry):
    span = min(wide, SPAN)
    if wide == span:
        return step(0, carry)
    return lax.fori_loop(0, wide // span, lambda i, c: step(pl.multiple_of(i * span, span), c), carry)


def lanes(base, offset, size):
    return pl.ds(pl.multiple_of(base + offset, 128), size) if not isinstance(base, int) else pl.ds(base + offset, size)


def pack_kernel(columns, me_ref, src_ref, tgt_ref, gf_ref, x_ref, y_ref, f_ref):
    f_ref[...] = pick(gf_ref[...], me_ref[0] % columns, src_ref.shape[1])
    x_ref[0] = src_ref[...]
    y_ref[0] = tgt_ref[...]


def lse_kernel(
    group, br, me_ref, x_ref, y_ref, lhs_ref, rhs_ref, yc_ref, p_ref, r_ref, lse_ref, sa_ref, sb_ref, acc_ref, m_ref
):
    me = me_ref[0]
    replicas, _, ns = x_ref.shape
    devices, features, nt = y_ref.shape
    rows, wide = p_ref.shape
    extra = lhs_ref.shape[1] - 3 * features
    lhs_ref[:, 3 * features :] = jnp.ones((rows, extra), BF16)
    for k in range(replicas):
        points = x_ref[k, :features, :].T
        for c in range(3):
            lhs_ref[k * ns : (k + 1) * ns, c * features : (c + 1) * features] = points
    yc_ref[features:, :] = jnp.ones((yc_ref.shape[0] - features, wide), BF16)
    for t in range(devices):
        cs = slice(t * nt, (t + 1) * nt)
        k = jnp.bitwise_xor(t, me)
        inner = k % group
        points = y_ref[(inner % 2) * (devices // 2) + (inner // 2) * replicas + k // group]
        yc_ref[:features, cs] = points
        points = points.astype(F32)
        square = fold(points * points) * -SQUARE
        value = points * CROSS
        high = value.astype(BF16)
        rest = value - high.astype(F32)
        mid = rest.astype(BF16)
        rhs_ref[:features, cs] = high
        rhs_ref[features : 2 * features, cs] = mid
        rhs_ref[2 * features : 3 * features, cs] = (rest - mid.astype(F32)).astype(BF16)
        rhs_ref[3 * features : 3 * features + 8, cs] = split3(square)
        rhs_ref[3 * features + 8 :, cs] = jnp.zeros((extra - 8, nt), BF16)
    scratch = (sa_ref, sb_ref)

    def scores(b):
        lb = lhs_ref[b * br : (b + 1) * br, :]
        s_ref = scratch[b % 2]

        def step(base, high):
            for u in range(0, min(wide, SPAN), 256):
                cs = lanes(base, u, 256)
                s = jnp.dot(lb, rhs_ref[:, cs], preferred_element_type=F32)
                s_ref[:, cs] = s
                high = jnp.maximum(high, jnp.maximum(s[:, :128], s[:, 128:]))
            return high

        return jnp.max(over(wide, step, jnp.full((br, 128), LOW, F32)), axis=1, keepdims=True)

    def exps(b, high):
        s_ref = scratch[b % 2]
        rs = slice(b * br, (b + 1) * br)
        hb = jnp.broadcast_to(high, (br, 128))

        def step(base, acc):
            for u in range(0, min(wide, SPAN), 128):
                cs = lanes(base, u, 128)
                e = jnp.exp2(s_ref[:, cs] - hb)
                p_ref[rs, cs] = e.astype(BF16)
                acc = acc + e
            return acc

        sums = jnp.sum(over(wide, step, jnp.zeros((br, 128), F32)), axis=1, keepdims=True)
        r_ref[rs, :] = jnp.broadcast_to(-(high + jnp.log2(sums)), (br, 128))
        return jnp.broadcast_to(1.0 / sums, (br, 128)).T[:1]

    count = rows // br
    inverse = []
    high = scores(0)
    for b in range(count):
        after = scores(b + 1) if b + 1 < count else None
        inverse.append(exps(b, high))
        high = after
    s = pulled(p_ref, jnp.concatenate(inverse, axis=1))
    lse_ref[...] = jnp.log2(jnp.maximum(s, TINY))

    @pl.when(jnp.min(s) < TINY)
    def _():
        acc_ref[...] = jnp.zeros(acc_ref.shape, F32)
        m_ref[...] = jnp.full(m_ref.shape, LOW, F32)

        def step(i, _):
            _, cs, v = tile_scores(i, lhs_ref, rhs_ref, r_ref)
            v = v.reshape(v.shape[0] // 8, 8, 128)
            old = m_ref[:, cs]
            new = jnp.maximum(old, jnp.max(v, axis=0))
            acc_ref[:, cs] = acc_ref[:, cs] * jnp.exp2(old - new) + fold3(jnp.exp2(v - new[None]))
            m_ref[:, cs] = new
            return 0

        lax.fori_loop(0, (rows // 128) * (wide // 128), step, 0)
        m = m_ref[...]
        top = jnp.max(m, axis=0, keepdims=True)
        lse_ref[...] = top + jnp.log2(fold(acc_ref[...] * jnp.exp2(m - top)))


def fold3(values):
    return jnp.sum(values, axis=0)


def tile_scores(i, lhs_ref, rhs_ref, r_ref):
    across = rhs_ref.shape[1] // 128
    rs = pl.ds(pl.multiple_of(i // across * 128, 128), 128)
    cs = pl.ds(pl.multiple_of(i % across * 128, 128), 128)
    return rs, cs, jnp.dot(lhs_ref[rs, :], rhs_ref[:, cs], preferred_element_type=F32) + r_ref[rs, :]


def pushed(p_ref, w):
    return fold(lax.dot_general(split3(w), p_ref[...], NT, preferred_element_type=F32))


def pulled(p_ref, y):
    return fold(jnp.dot(split3(y), p_ref[...], preferred_element_type=F32))


def plan_kernel(count, shift, *refs):
    parts, (lhs_ref, rhs_ref, r_ref, old_ref, p_ref, scale_ref, a_ref, s_ref) = refs[:count], refs[count:]
    top = functools.reduce(jnp.maximum, [q[...] for q in parts])
    c = shift - top - jnp.log2(sum(jnp.exp2(q[...] - top) for q in parts))
    rows, wide = p_ref.shape
    plain = jnp.max(c) <= LIMIT
    scale_ref[...] = jnp.exp2(jnp.minimum(c, LIMIT))

    @pl.when(jnp.logical_not(plain))
    def _():
        scale_ref[...] = c

        def step(i, _):
            rs, cs, v = tile_scores(i, lhs_ref, rhs_ref, r_ref)
            p_ref[rs, cs] = jnp.exp2(v + scale_ref[:, cs]).astype(BF16)
            return 0

        lax.fori_loop(0, (rows // 128) * (wide // 128), step, 0)
        scale_ref[...] = jnp.ones((1, wide), F32)

    scale = scale_ref[...]
    a = 1.0 / pushed(p_ref, scale)
    a_ref[...] = a
    s_ref[...] = scale * pulled(p_ref, a)


def rhs_kernel(count, ratio, *refs):
    parts, (p_ref, scale_ref, gf_ref, g_ref, b_ref, cm_ref, m_ref, out_ref) = refs[:count], refs[count:]
    s = sum(q[...] for q in parts)
    b = ratio / s
    b_ref[...] = b
    cm_ref[...] = b * s

    scale = scale_ref[...]
    m = pushed(p_ref, scale * b)
    m_ref[...] = m
    out_ref[...] = g_ref[...] - b * scale * pulled(p_ref, gf_ref[...] / m)


def advance(parts, b, cm, dual, residual, direction):
    image = (1.0 + TAU) * cm * direction - b * sum(q[...] for q in parts)
    alpha = total(residual * residual) / total(direction * image)
    return alpha, dual + alpha * direction, residual - alpha * image


def cg_kernel(count, first, *refs):
    parts, refs = refs[:count], refs[count:]
    p_ref, scale_ref, a_ref, m_ref, b_ref, cm_ref = refs[:6]
    b = b_ref[...]
    if first:
        out = refs[6:]
        direction = sum(q[...] for q in parts)
        residual = direction
        dual = jnp.zeros_like(direction)
        mix = jnp.zeros(a_ref.shape, F32)
    else:
        dual_ref, res_ref, dir_ref, q_ref, mix_ref = refs[6:11]
        out = refs[11:]
        old = res_ref[...]
        before = dir_ref[...]
        alpha, dual, residual = advance(parts, b, cm_ref[...], dual_ref[...], old, before)
        direction = residual + total(residual * residual) / total(old * old) * before
        mix = mix_ref[...] + alpha * q_ref[...]
    dual_out, res_out, dir_out, q_out, mix_out, u_out = out
    dual_out[...] = dual
    res_out[...] = residual
    dir_out[...] = direction
    mix_out[...] = mix

    scale = scale_ref[...]
    q = pushed(p_ref, scale * b * direction)
    q_out[...] = q
    u_out[...] = scale * pulled(p_ref, a_ref[...] * q / m_ref[...])


def grad_kernel(count, group, *refs):
    parts, refs = refs[:count], refs[count:]
    me_ref, p_ref, scale_ref, a_ref, m_ref, b_ref, cm_ref, dual_ref, res_ref, dir_ref, q_ref, mix_ref = refs[:12]
    gf_ref, x_ref, yc_ref, srca_ref, srcb_ref, tgt_ref, step_ref = refs[12:19]
    wa_ref, wb_ref, va_ref, vb_ref, ad_ref, da_ref, db_ref = refs[19:]
    me = me_ref[0]
    replicas, _, ns = x_ref.shape
    features = srca_ref.shape[0]
    nt = tgt_ref.shape[2]
    b = b_ref[...]
    cm = cm_ref[...]
    old = res_ref[...]
    before = dir_ref[...]
    alpha, dual, residual = advance(parts, b, cm, dual_ref[...], old, before)
    norm = total(residual * residual)
    direction = residual + norm / total(old * old) * before
    a = a_ref[...]
    m = m_ref[...]
    mix = mix_ref[...] + alpha * q_ref[...]
    b = b * scale_ref[...]
    q = pushed(p_ref, b * direction)
    ad_ref[...] = down(a)
    da_ref[...] = down((gf_ref[...] / a - mix) / m)
    db_ref[...] = down(-q / m)
    step_ref[0:1, :] = jnp.broadcast_to(norm, (1, 128))
    step_ref[1:2, :] = jnp.broadcast_to(total((1.0 + TAU) * cm * direction * direction), (1, 128))
    taken = total(a * q * q / m)
    wide = b.shape[1]
    half = group * nt
    base = (me // group) * half

    def weigh(rows, source, bs, duals, dirs, outs):
        plan = source.astype(F32) * (ad_ref[rows, :] * bs)
        outs[0][...] = (plan * (da_ref[rows, :] + duals)).astype(BF16)
        outs[1][...] = (plan * (db_ref[rows, :] + dirs)).astype(BF16)

    for u in range(wide // 128):
        cs = slice(u * 128, (u + 1) * 128)
        weigh(slice(0, ns), p_ref[:ns, cs], b[:, cs], dual[:, cs], direction[:, cs], (wa_ref.at[:, cs], wb_ref.at[:, cs]))
    own = x_ref[0, :features, :].astype(F32)
    for w_ref, out_ref in ((wa_ref, srca_ref), (wb_ref, srcb_ref)):
        out = lax.dot_general(yc_ref[...], w_ref[...], NT, preferred_element_type=F32)
        out_ref[...] = 2.0 * (own * out[features : features + 1] - out[:features])

    b, dual, direction = [pick(v, me // group, half) for v in (b, dual, direction)]
    for u in range(half // 128):
        cs = slice(u * 128, (u + 1) * 128)
        cd = pl.ds(pl.multiple_of(base + u * 128, 128), 128)
        weigh(slice(None), p_ref[:, cd], b[:, cs], dual[:, cs], direction[:, cs], (va_ref.at[:, cs], vb_ref.at[:, cs]))
    mine = yc_ref[:features, pl.ds(pl.multiple_of(base, 128), half)].astype(F32)
    ones = jnp.ones((8, va_ref.shape[0]), BF16)
    for c, w_ref in enumerate((va_ref, vb_ref)):
        sums = jnp.zeros((features, half), F32)
        for k in range(replicas):
            rows = slice(k * ns, (k + 1) * ns)
            sums = sums + jnp.dot(x_ref[k, :features, :], w_ref[rows, :], preferred_element_type=F32)
        part = 2.0 * (mine * jnp.dot(ones, w_ref[...], preferred_element_type=F32)[:1] - sums)
        for k in range(group):
            slot = jnp.bitwise_xor(k, me % group)
            tgt_ref[slot, c * features : (c + 1) * features, :] = part[:, k * nt : (k + 1) * nt]
    for k in range(group):
        tgt_ref[k, 2 * features :, :] = jnp.broadcast_to(taken, (8, nt))


def last_kernel(count, *refs):
    parts, (srca_ref, srcb_ref, step_ref, src_ref, tgt_ref) = refs[:count], refs[count:]
    features = src_ref.shape[0]
    rows = sum(q[0] for q in parts)
    alpha = step_ref[0:1, 0:1] / (step_ref[1:2, 0:1] - rows[2 * features : 2 * features + 1, 0:1])
    src_ref[...] = srca_ref[...] + alpha * srcb_ref[...]
    tgt_ref[...] = rows[:features] + alpha * rows[features : 2 * features]


def pick(vector, index, size):
    out = vector[:, :size]
    for k in range(1, vector.shape[1] // size):
        out = jnp.where(index == k, vector[:, k * size : (k + 1) * size], out)
    return out


def call(kernel, operands, outs, scratch, smem=(), limit=24, alias={}):
    return pl.pallas_call(
        kernel,
        out_shape=outs,
        in_specs=[SMEM if i in smem else VMEM for i in range(len(operands))],
        out_specs=[VMEM] * len(outs),
        scratch_shapes=scratch,
        input_output_aliases=alias,
        compiler_params=pltpu.CompilerParams(vmem_limit_bytes=limit * 1024 * 1024),
    )(*operands)


def body(src_points, tgt_points, grad_f, grad_g):
    rows_axis, cols_axis = lax.axis_size("row"), lax.axis_size("col")
    devices = rows_axis * cols_axis
    features, ns = src_points.shape
    nt = tgt_points.shape[1]
    wide = devices * nt
    group = 2
    while group < devices and devices // group * ns * wide > ELEMENTS:
        group *= 2
    replicas = devices // group
    rows = replicas * ns
    row, col = lax.axis_index("row"), lax.axis_index("col")
    me = row * cols_axis + col
    me_ref = me.astype(jnp.int32).reshape(1)

    def swap(value, mask):
        return lax.ppermute(value, AXES, [(i, i ^ mask) for i in range(devices)])

    bits = [1 << i for i in range(1, group.bit_length() - 1)]
    stages = [[1]]
    for i in range(0, len(bits), 2):
        pair = bits[i : i + 2]
        stages.append(([pair[0] | pair[1]] if len(pair) == 2 else []) + pair[::-1])

    def exchange(value, combine):
        for stage in stages[:-1]:
            value = combine([value] + [swap(value, mask) for mask in stage])
        return [value] + [swap(value, mask) for mask in stages[-1]]

    x, y, gf = call(
        functools.partial(pack_kernel, cols_axis),
        (me_ref, src_points, tgt_points, grad_f.reshape(1, -1)),
        (
            jax.ShapeDtypeStruct((1, features, ns), BF16),
            jax.ShapeDtypeStruct((1, features, nt), BF16),
            jax.ShapeDtypeStruct((1, ns), F32),
        ),
        [],
        smem=(0,),
        limit=4,
    )
    mask = group
    while mask < devices:
        y = jnp.concatenate([y, swap(y if mask > group else tgt_points[None], mask)])
        x = jnp.concatenate([x, swap(x if mask > group else src_points[None], mask)])
        mask *= 2
    for stage in stages[1:] + stages[:1]:
        sent = {0: y} | {mask // stage[-1]: swap(y, mask) for mask in stage}
        y = jnp.concatenate([sent[k] for k in range(len(sent))])
    own = (jnp.arange(cols_axis)[None, :, None] == col) & (row % (group // cols_axis) == 0)
    g = jnp.where(own, grad_g.reshape(rows_axis, 1, nt), 0.0).reshape(1, wide)

    br = min(256, rows, ELEMENTS // 4 // wide)
    vec = jax.ShapeDtypeStruct((1, wide), F32)
    line = jax.ShapeDtypeStruct((1, rows), F32)
    acc = pltpu.VMEM((8, wide), F32)
    block = pltpu.VMEM((br, wide), F32)
    depth = -(-(3 * features + 8) // 128) * 128
    plan = jax.ShapeDtypeStruct((rows, wide), BF16)
    lhs, rhs, yc, p, r, lse = call(
        functools.partial(lse_kernel, group, br),
        (me_ref, x, y),
        (
            jax.ShapeDtypeStruct((rows, depth), BF16),
            jax.ShapeDtypeStruct((depth, wide), BF16),
            jax.ShapeDtypeStruct((features + 16, wide), BF16),
            plan,
            jax.ShapeDtypeStruct((rows, 128), F32),
            vec,
        ),
        [block, block, acc, acc],
        smem=(0,),
        limit=32,
    )

    lse, gf = lax.optimization_barrier((lse, gf))
    mask = group
    while mask < devices:
        gf = jnp.concatenate([gf, swap(gf, mask)])
        mask *= 2
    gf = gf.reshape(1, rows)

    def join(values):
        top = functools.reduce(jnp.maximum, values)
        return top + jnp.log2(sum(jnp.exp2(v - top) for v in values))

    parts = exchange(lse, join)
    count = len(parts)
    p, scale, a, s = call(
        functools.partial(plan_kernel, count, math.log2(ns / nt)),
        (*parts, lhs, rhs, r, p),
        (plan, vec, line, vec),
        [],
        alias={count + 3: 0},
    )
    parts = exchange(s, sum)
    b, cm, m, u = call(
        functools.partial(rhs_kernel, count, ns / nt),
        (*parts, p, scale, gf, g),
        (vec, vec, line, vec),
        [],
    )
    state = ()
    for step in range(CG - 1):
        parts = exchange(u, sum)
        *state, u = call(
            functools.partial(cg_kernel, count, step == 0),
            (*parts, p, scale, a, m, b, cm, *state),
            (vec, vec, vec, line, line, vec),
            [],
        )
    parts = exchange(u, sum)
    grad = jax.ShapeDtypeStruct((features, ns), F32)
    srca, srcb, part, scalars = call(
        functools.partial(grad_kernel, count, group),
        (*parts, me_ref, p, scale, a, m, b, cm, *state, gf, x, yc),
        (
            grad,
            grad,
            jax.ShapeDtypeStruct((group, 2 * features + 8, nt), F32),
            jax.ShapeDtypeStruct((8, 128), F32),
        ),
        [pltpu.VMEM((ns, wide), BF16)] * 2
        + [pltpu.VMEM((rows, group * nt), BF16)] * 2
        + [pltpu.VMEM((rows, 128), F32)] * 3,
        smem=(count,),
    )
    for stage in stages:
        size = len(stage) + 1
        part = part.reshape(part.shape[0] // size, size, *part.shape[1:])
        pieces = [part[:, 0]] + [swap(part[:, mask // stage[-1]], mask) for mask in stage]
        part = sum(pieces[1:], pieces[0]) if stage is not stages[-1] else part
    return call(
        functools.partial(last_kernel, len(pieces)),
        (*pieces, srca, srcb, scalars),
        (grad, jax.ShapeDtypeStruct((features, nt), F32)),
        [],
    )


def solution(mesh):
    in_specs = (P(None, ("row", "col")), P(None, ("col", "row")), P("row"), P("col"))
    out_specs = (P(None, ("row", "col")), P(None, ("col", "row")))

    return jax.shard_map(body, mesh=mesh, in_specs=in_specs, out_specs=out_specs, check_vma=False)
```

```python
import functools
import math

import jax
import jax.numpy as jnp
from jax import lax
from jax.experimental import pallas as pl
from jax.experimental.pallas import tpu as pltpu
from jax.sharding import PartitionSpec as P


CG = 3
EPS = 4.0
TAU = 0.1
AXES = ("row", "col")
LOW = -3.0e38
TINY = 2.0**-80
LIMIT = 80.0
SPAN = 4096
ELEMENTS = 4 * 1024 * 1024
LOG2E = math.log2(math.e)
CROSS = 2.0 * LOG2E / EPS
SQUARE = LOG2E / EPS
F32 = jnp.float32
BF16 = jnp.bfloat16
NT = (((1,), (1,)), ((), ()))
VMEM = pl.BlockSpec(memory_space=pltpu.VMEM)
SMEM = pl.BlockSpec(memory_space=pltpu.SMEM)


def split3(vector):
    high = vector.astype(BF16).astype(F32)
    rest = vector - high
    mid = rest.astype(BF16).astype(F32)
    low = rest - mid
    shape = (8, vector.shape[1])
    line = lax.broadcasted_iota(jnp.int32, shape, 0)
    zero = jnp.zeros(shape, F32)
    rows = jnp.where(line == 0, high, jnp.where(line == 1, mid, jnp.where(line == 2, low, zero)))
    return rows.astype(BF16)


def total(vector):
    return jnp.sum(vector, axis=1, keepdims=True)


def fold(rows):
    return jnp.sum(rows, axis=0, keepdims=True)


def down(vector):
    return jnp.broadcast_to(vector, (128, vector.shape[1])).T


def over(wide, step, carry):
    span = min(wide, SPAN)
    if wide == span:
        return step(0, carry)
    return lax.fori_loop(0, wide // span, lambda i, c: step(pl.multiple_of(i * span, span), c), carry)


def lanes(base, offset, size):
    return pl.ds(pl.multiple_of(base + offset, 128), size) if not isinstance(base, int) else pl.ds(base + offset, size)


def pack_kernel(columns, me_ref, src_ref, tgt_ref, gf_ref, x_ref, y_ref, f_ref):
    f_ref[...] = pick(gf_ref[...], me_ref[0] % columns, src_ref.shape[1])
    x_ref[0] = src_ref[...]
    y_ref[0] = tgt_ref[...]


def lse_kernel(
    group, br, me_ref, x_ref, y_ref, lhs_ref, rhs_ref, yc_ref, p_ref, pt_ref, r_ref, lse_ref, sa_ref, sb_ref, acc_ref, m_ref
):
    me = me_ref[0]
    replicas, _, ns = x_ref.shape
    devices, features, nt = y_ref.shape
    rows, wide = p_ref.shape
    extra = lhs_ref.shape[1] - 3 * features
    lhs_ref[:, 3 * features :] = jnp.ones((rows, extra), BF16)
    for k in range(replicas):
        points = x_ref[k, :features, :].T
        for c in range(3):
            lhs_ref[k * ns : (k + 1) * ns, c * features : (c + 1) * features] = points
    yc_ref[features:, :] = jnp.ones((yc_ref.shape[0] - features, wide), BF16)
    for t in range(devices):
        cs = slice(t * nt, (t + 1) * nt)
        k = jnp.bitwise_xor(t, me)
        inner = k % group
        points = y_ref[(inner % 2) * (devices // 2) + (inner // 2) * replicas + k // group]
        yc_ref[:features, cs] = points
        points = points.astype(F32)
        square = fold(points * points) * -SQUARE
        value = points * CROSS
        high = value.astype(BF16)
        rest = value - high.astype(F32)
        mid = rest.astype(BF16)
        rhs_ref[:features, cs] = high
        rhs_ref[features : 2 * features, cs] = mid
        rhs_ref[2 * features : 3 * features, cs] = (rest - mid.astype(F32)).astype(BF16)
        rhs_ref[3 * features : 3 * features + 8, cs] = split3(square)
        rhs_ref[3 * features + 8 :, cs] = jnp.zeros((extra - 8, nt), BF16)
    scratch = (sa_ref, sb_ref)

    def scores(b):
        lb = lhs_ref[b * br : (b + 1) * br, :]
        s_ref = scratch[b % 2]

        def step(base, high):
            for u in range(0, min(wide, SPAN), 256):
                cs = lanes(base, u, 256)
                s = jnp.dot(lb, rhs_ref[:, cs], preferred_element_type=F32)
                s_ref[:, cs] = s
                high = jnp.maximum(high, jnp.maximum(s[:, :128], s[:, 128:]))
            return high

        return jnp.max(over(wide, step, jnp.full((br, 128), LOW, F32)), axis=1, keepdims=True)

    def exps(b, high):
        s_ref = scratch[b % 2]
        rs = slice(b * br, (b + 1) * br)
        hb = jnp.broadcast_to(high, (br, 128))

        def step(base, acc):
            for u in range(0, min(wide, SPAN), 128):
                cs = lanes(base, u, 128)
                e = jnp.exp2(s_ref[:, cs] - hb)
                rounded = e.astype(BF16)
                p_ref[rs, cs] = rounded
                pt_ref[cs, rs] = rounded.T
                acc = acc + e
            return acc

        sums = jnp.sum(over(wide, step, jnp.zeros((br, 128), F32)), axis=1, keepdims=True)
        r_ref[rs, :] = jnp.broadcast_to(-(high + jnp.log2(sums)), (br, 128))
        return jnp.broadcast_to(1.0 / sums, (br, 128)).T[:1]

    count = rows // br
    inverse = []
    high = scores(0)
    for b in range(count):
        after = scores(b + 1) if b + 1 < count else None
        inverse.append(exps(b, high))
        high = after
    s = pulled(p_ref, jnp.concatenate(inverse, axis=1))
    lse_ref[...] = jnp.log2(jnp.maximum(s, TINY))

    @pl.when(jnp.min(s) < TINY)
    def _():
        acc_ref[...] = jnp.zeros(acc_ref.shape, F32)
        m_ref[...] = jnp.full(m_ref.shape, LOW, F32)

        def step(i, _):
            _, cs, v = tile_scores(i, lhs_ref, rhs_ref, r_ref)
            v = v.reshape(v.shape[0] // 8, 8, 128)
            old = m_ref[:, cs]
            new = jnp.maximum(old, jnp.max(v, axis=0))
            acc_ref[:, cs] = acc_ref[:, cs] * jnp.exp2(old - new) + fold3(jnp.exp2(v - new[None]))
            m_ref[:, cs] = new
            return 0

        lax.fori_loop(0, (rows // 128) * (wide // 128), step, 0)
        m = m_ref[...]
        top = jnp.max(m, axis=0, keepdims=True)
        lse_ref[...] = top + jnp.log2(fold(acc_ref[...] * jnp.exp2(m - top)))


def fold3(values):
    return jnp.sum(values, axis=0)


def tile_scores(i, lhs_ref, rhs_ref, r_ref):
    across = rhs_ref.shape[1] // 128
    rs = pl.ds(pl.multiple_of(i // across * 128, 128), 128)
    cs = pl.ds(pl.multiple_of(i % across * 128, 128), 128)
    return rs, cs, jnp.dot(lhs_ref[rs, :], rhs_ref[:, cs], preferred_element_type=F32) + r_ref[rs, :]


def pushed(pt_ref, w):
    return fold(jnp.dot(split3(w), pt_ref[...], preferred_element_type=F32))


def pulled(p_ref, y):
    return fold(jnp.dot(split3(y), p_ref[...], preferred_element_type=F32))


def plan_kernel(count, shift, *refs):
    parts, (lhs_ref, rhs_ref, r_ref, old_ref, turned_ref, p_ref, pt_ref, scale_ref, a_ref, s_ref) = refs[:count], refs[count:]
    top = functools.reduce(jnp.maximum, [q[...] for q in parts])
    c = shift - top - jnp.log2(sum(jnp.exp2(q[...] - top) for q in parts))
    rows, wide = p_ref.shape
    plain = jnp.max(c) <= LIMIT
    scale_ref[...] = jnp.exp2(jnp.minimum(c, LIMIT))

    @pl.when(jnp.logical_not(plain))
    def _():
        scale_ref[...] = c

        def step(i, _):
            rs, cs, v = tile_scores(i, lhs_ref, rhs_ref, r_ref)
            rounded = jnp.exp2(v + scale_ref[:, cs]).astype(BF16)
            p_ref[rs, cs] = rounded
            pt_ref[cs, rs] = rounded.T
            return 0

        lax.fori_loop(0, (rows // 128) * (wide // 128), step, 0)
        scale_ref[...] = jnp.ones((1, wide), F32)

    scale = scale_ref[...]
    a = 1.0 / pushed(pt_ref, scale)
    a_ref[...] = a
    s_ref[...] = scale * pulled(p_ref, a)


def rhs_kernel(count, ratio, *refs):
    parts, (p_ref, pt_ref, scale_ref, gf_ref, g_ref, b_ref, cm_ref, m_ref, out_ref) = refs[:count], refs[count:]
    s = sum(q[...] for q in parts)
    b = ratio / s
    b_ref[...] = b
    cm_ref[...] = b * s

    scale = scale_ref[...]
    m = pushed(pt_ref, scale * b)
    m_ref[...] = m
    out_ref[...] = g_ref[...] - b * scale * pulled(p_ref, gf_ref[...] / m)


def advance(parts, b, cm, dual, residual, direction):
    image = (1.0 + TAU) * cm * direction - b * sum(q[...] for q in parts)
    alpha = total(residual * residual) / total(direction * image)
    return alpha, dual + alpha * direction, residual - alpha * image


def cg_kernel(count, first, *refs):
    parts, refs = refs[:count], refs[count:]
    p_ref, pt_ref, scale_ref, a_ref, m_ref, b_ref, cm_ref = refs[:7]
    b = b_ref[...]
    if first:
        out = refs[7:]
        direction = sum(q[...] for q in parts)
        residual = direction
        dual = jnp.zeros_like(direction)
        mix = jnp.zeros(a_ref.shape, F32)
    else:
        dual_ref, res_ref, dir_ref, q_ref, mix_ref = refs[7:12]
        out = refs[12:]
        old = res_ref[...]
        before = dir_ref[...]
        alpha, dual, residual = advance(parts, b, cm_ref[...], dual_ref[...], old, before)
        direction = residual + total(residual * residual) / total(old * old) * before
        mix = mix_ref[...] + alpha * q_ref[...]
    dual_out, res_out, dir_out, q_out, mix_out, u_out = out
    dual_out[...] = dual
    res_out[...] = residual
    dir_out[...] = direction
    mix_out[...] = mix

    scale = scale_ref[...]
    q = pushed(pt_ref, scale * b * direction)
    q_out[...] = q
    u_out[...] = scale * pulled(p_ref, a_ref[...] * q / m_ref[...])


def grad_kernel(count, group, *refs):
    parts, refs = refs[:count], refs[count:]
    me_ref, p_ref, pt_ref, scale_ref, a_ref, m_ref, b_ref, cm_ref, dual_ref, res_ref, dir_ref, q_ref, mix_ref = refs[:13]
    gf_ref, x_ref, yc_ref, srca_ref, srcb_ref, tgt_ref, step_ref = refs[13:20]
    wa_ref, wb_ref, va_ref, vb_ref, ad_ref, da_ref, db_ref = refs[20:]
    me = me_ref[0]
    replicas, _, ns = x_ref.shape
    features = srca_ref.shape[0]
    nt = tgt_ref.shape[2]
    b = b_ref[...]
    cm = cm_ref[...]
    old = res_ref[...]
    before = dir_ref[...]
    alpha, dual, residual = advance(parts, b, cm, dual_ref[...], old, before)
    norm = total(residual * residual)
    direction = residual + norm / total(old * old) * before
    a = a_ref[...]
    m = m_ref[...]
    mix = mix_ref[...] + alpha * q_ref[...]
    b = b * scale_ref[...]
    q = pushed(pt_ref, b * direction)
    ad_ref[...] = down(a)
    da_ref[...] = down((gf_ref[...] / a - mix) / m)
    db_ref[...] = down(-q / m)
    step_ref[0:1, :] = jnp.broadcast_to(norm, (1, 128))
    step_ref[1:2, :] = jnp.broadcast_to(total((1.0 + TAU) * cm * direction * direction), (1, 128))
    taken = total(a * q * q / m)
    wide = b.shape[1]
    half = group * nt
    base = (me // group) * half

    def weigh(rows, source, bs, duals, dirs, outs):
        plan = source.astype(F32) * (ad_ref[rows, :] * bs)
        outs[0][...] = (plan * (da_ref[rows, :] + duals)).astype(BF16)
        outs[1][...] = (plan * (db_ref[rows, :] + dirs)).astype(BF16)

    for u in range(wide // 128):
        cs = slice(u * 128, (u + 1) * 128)
        weigh(slice(0, ns), p_ref[:ns, cs], b[:, cs], dual[:, cs], direction[:, cs], (wa_ref.at[:, cs], wb_ref.at[:, cs]))
    own = x_ref[0, :features, :].astype(F32)
    for w_ref, out_ref in ((wa_ref, srca_ref), (wb_ref, srcb_ref)):
        out = lax.dot_general(yc_ref[...], w_ref[...], NT, preferred_element_type=F32)
        out_ref[...] = 2.0 * (own * out[features : features + 1] - out[:features])

    b, dual, direction = [pick(v, me // group, half) for v in (b, dual, direction)]
    for u in range(half // 128):
        cs = slice(u * 128, (u + 1) * 128)
        cd = pl.ds(pl.multiple_of(base + u * 128, 128), 128)
        weigh(slice(None), p_ref[:, cd], b[:, cs], dual[:, cs], direction[:, cs], (va_ref.at[:, cs], vb_ref.at[:, cs]))
    mine = yc_ref[:features, pl.ds(pl.multiple_of(base, 128), half)].astype(F32)
    ones = jnp.ones((8, va_ref.shape[0]), BF16)
    for c, w_ref in enumerate((va_ref, vb_ref)):
        sums = jnp.zeros((features, half), F32)
        for k in range(replicas):
            rows = slice(k * ns, (k + 1) * ns)
            sums = sums + jnp.dot(x_ref[k, :features, :], w_ref[rows, :], preferred_element_type=F32)
        part = 2.0 * (mine * jnp.dot(ones, w_ref[...], preferred_element_type=F32)[:1] - sums)
        for k in range(group):
            slot = jnp.bitwise_xor(k, me % group)
            tgt_ref[slot, c * features : (c + 1) * features, :] = part[:, k * nt : (k + 1) * nt]
    for k in range(group):
        tgt_ref[k, 2 * features :, :] = jnp.broadcast_to(taken, (8, nt))


def last_kernel(count, *refs):
    parts, (srca_ref, srcb_ref, step_ref, src_ref, tgt_ref) = refs[:count], refs[count:]
    features = src_ref.shape[0]
    rows = sum(q[0] for q in parts)
    alpha = step_ref[0:1, 0:1] / (step_ref[1:2, 0:1] - rows[2 * features : 2 * features + 1, 0:1])
    src_ref[...] = srca_ref[...] + alpha * srcb_ref[...]
    tgt_ref[...] = rows[:features] + alpha * rows[features : 2 * features]


def pick(vector, index, size):
    out = vector[:, :size]
    for k in range(1, vector.shape[1] // size):
        out = jnp.where(index == k, vector[:, k * size : (k + 1) * size], out)
    return out


def call(kernel, operands, outs, scratch, smem=(), limit=24, alias={}):
    return pl.pallas_call(
        kernel,
        out_shape=outs,
        in_specs=[SMEM if i in smem else VMEM for i in range(len(operands))],
        out_specs=[VMEM] * len(outs),
        scratch_shapes=scratch,
        input_output_aliases=alias,
        compiler_params=pltpu.CompilerParams(vmem_limit_bytes=limit * 1024 * 1024),
    )(*operands)


def body(src_points, tgt_points, grad_f, grad_g):
    rows_axis, cols_axis = lax.axis_size("row"), lax.axis_size("col")
    devices = rows_axis * cols_axis
    features, ns = src_points.shape
    nt = tgt_points.shape[1]
    wide = devices * nt
    group = 2
    while group < devices and devices // group * ns * wide > ELEMENTS:
        group *= 2
    replicas = devices // group
    rows = replicas * ns
    row, col = lax.axis_index("row"), lax.axis_index("col")
    me = row * cols_axis + col
    me_ref = me.astype(jnp.int32).reshape(1)

    def swap(value, mask):
        return lax.ppermute(value, AXES, [(i, i ^ mask) for i in range(devices)])

    bits = [1 << i for i in range(1, group.bit_length() - 1)]
    stages = [[1]]
    for i in range(0, len(bits), 2):
        pair = bits[i : i + 2]
        stages.append(([pair[0] | pair[1]] if len(pair) == 2 else []) + pair[::-1])

    def exchange(value, combine):
        for stage in stages[:-1]:
            value = combine([value] + [swap(value, mask) for mask in stage])
        return [value] + [swap(value, mask) for mask in stages[-1]]

    x, y, gf = call(
        functools.partial(pack_kernel, cols_axis),
        (me_ref, src_points, tgt_points, grad_f.reshape(1, -1)),
        (
            jax.ShapeDtypeStruct((1, features, ns), BF16),
            jax.ShapeDtypeStruct((1, features, nt), BF16),
            jax.ShapeDtypeStruct((1, ns), F32),
        ),
        [],
        smem=(0,),
        limit=4,
    )
    mask = group
    while mask < devices:
        y = jnp.concatenate([y, swap(y if mask > group else tgt_points[None], mask)])
        x = jnp.concatenate([x, swap(x if mask > group else src_points[None], mask)])
        mask *= 2
    for stage in stages[1:] + stages[:1]:
        sent = {0: y} | {mask // stage[-1]: swap(y, mask) for mask in stage}
        y = jnp.concatenate([sent[k] for k in range(len(sent))])
    own = (jnp.arange(cols_axis)[None, :, None] == col) & (row % (group // cols_axis) == 0)
    g = jnp.where(own, grad_g.reshape(rows_axis, 1, nt), 0.0).reshape(1, wide)

    br = min(256, rows, ELEMENTS // 4 // wide)
    vec = jax.ShapeDtypeStruct((1, wide), F32)
    line = jax.ShapeDtypeStruct((1, rows), F32)
    acc = pltpu.VMEM((8, wide), F32)
    block = pltpu.VMEM((br, wide), F32)
    depth = -(-(3 * features + 8) // 128) * 128
    plan = jax.ShapeDtypeStruct((rows, wide), BF16)
    turned = jax.ShapeDtypeStruct((wide, rows), BF16)
    lhs, rhs, yc, p, pt, r, lse = call(
        functools.partial(lse_kernel, group, br),
        (me_ref, x, y),
        (
            jax.ShapeDtypeStruct((rows, depth), BF16),
            jax.ShapeDtypeStruct((depth, wide), BF16),
            jax.ShapeDtypeStruct((features + 16, wide), BF16),
            plan,
            turned,
            jax.ShapeDtypeStruct((rows, 128), F32),
            vec,
        ),
        [block, block, acc, acc],
        smem=(0,),
        limit=32,
    )

    lse, gf = lax.optimization_barrier((lse, gf))
    mask = group
    while mask < devices:
        gf = jnp.concatenate([gf, swap(gf, mask)])
        mask *= 2
    gf = gf.reshape(1, rows)

    def join(values):
        top = functools.reduce(jnp.maximum, values)
        return top + jnp.log2(sum(jnp.exp2(v - top) for v in values))

    parts = exchange(lse, join)
    count = len(parts)
    p, pt, scale, a, s = call(
        functools.partial(plan_kernel, count, math.log2(ns / nt)),
        (*parts, lhs, rhs, r, p, pt),
        (plan, turned, vec, line, vec),
        [],
        alias={count + 3: 0, count + 4: 1},
    )
    parts = exchange(s, sum)
    b, cm, m, u = call(
        functools.partial(rhs_kernel, count, ns / nt),
        (*parts, p, pt, scale, gf, g),
        (vec, vec, line, vec),
        [],
    )
    state = ()
    for step in range(CG - 1):
        parts = exchange(u, sum)
        *state, u = call(
            functools.partial(cg_kernel, count, step == 0),
            (*parts, p, pt, scale, a, m, b, cm, *state),
            (vec, vec, vec, line, line, vec),
            [],
        )
    parts = exchange(u, sum)
    grad = jax.ShapeDtypeStruct((features, ns), F32)
    srca, srcb, part, scalars = call(
        functools.partial(grad_kernel, count, group),
        (*parts, me_ref, p, pt, scale, a, m, b, cm, *state, gf, x, yc),
        (
            grad,
            grad,
            jax.ShapeDtypeStruct((group, 2 * features + 8, nt), F32),
            jax.ShapeDtypeStruct((8, 128), F32),
        ),
        [pltpu.VMEM((ns, wide), BF16)] * 2
        + [pltpu.VMEM((rows, group * nt), BF16)] * 2
        + [pltpu.VMEM((rows, 128), F32)] * 3,
        smem=(count,),
        limit=26,
    )
    for stage in stages:
        size = len(stage) + 1
        part = part.reshape(part.shape[0] // size, size, *part.shape[1:])
        pieces = [part[:, 0]] + [swap(part[:, mask // stage[-1]], mask) for mask in stage]
        part = sum(pieces[1:], pieces[0]) if stage is not stages[-1] else part
    return call(
        functools.partial(last_kernel, len(pieces)),
        (*pieces, srca, srcb, scalars),
        (grad, jax.ShapeDtypeStruct((features, nt), F32)),
        [],
    )


def solution(mesh):
    in_specs = (P(None, ("row", "col")), P(None, ("col", "row")), P("row"), P("col"))
    out_specs = (P(None, ("row", "col")), P(None, ("col", "row")))

    return jax.shard_map(body, mesh=mesh, in_specs=in_specs, out_specs=out_specs, check_vma=False)
```
